128 devices in a mesh: dp: 8 (over z, core), node: 16 (over x, y).
Axes of the slice: x: 4, y: 4, z: 4, core: 2. Of those that a mesh axis runs over, the one named last changes fastest.
Arguments:
- vertex_embeddings: bfloat16 [8, 8192, 768], P('dp', 'node'), may hold values from -12 to 12
- incoming_adjoint: bfloat16 [8, 8192, 768], P('dp', 'node'), may hold values from -6 to 6
- asking_projector_matrix: bfloat16 [768, 768], replicated, may hold values from -0.21875 to 0.21875
- lookup_projector_matrix: bfloat16 [768, 768], replicated, may hold values from -0.21875 to 0.21875
- content_projector_matrix: bfloat16 [768, 768], replicated, may hold values from -0.21875 to 0.21875
- final_projector_matrix: bfloat16 [768, 768], replicated, may hold values from -0.21875 to 0.21875
- grouped_vertex_permutation: int32 [8, 8192], P('dp'), may hold values from 0 to 8191, as said below
- listed_tiles: int32 [8, 32, 64, 4], P('dp'), may hold values from 0 to 63, as said below
- active_tile_tally: int32 [8, 32, 64], P('dp'), may hold values from 1 to 4, as said below
Outputs:
- sublayer_yield: bfloat16 [8, 8192, 768], P('dp', 'node')
- embedding_derivative: bfloat16 [8, 8192, 768], P('dp', 'node')
- grad_query: float32 [768, 768], replicated
- grad_key: float32 [768, 768], replicated
- grad_value: float32 [768, 768], replicated
- grad_out: float32 [768, 768], replicated
The draws below stay inside these ranges and needn't reach their ends.
Inputs may be any that keep to these rules, and one draw needn't show every extreme that they name: `grouped_vertex_permutation`: each subgraph's row is a permutation of the 8192 nodes. listed_tiles[g, h, b, :] are 4 distinct key block numbers, the first of them b. `active_tile_tally`: for every subgraph and head some query block has 4.
All inputs are finite; a program needn't handle non-finite values.
Results may differ from the reference program's by a relative error of at most 0.015.
The reference program's roundings to bfloat16 on the way count: a program that leaves them out, or rounds other values in their place, can miss the bound.
Values may be sent and summed in bfloat16 or wider, within the bound.
No kernel may reach another device: no remote copies, remote signals or barrier semaphores. Data moves between devices by JAX's collectives and lax.ppermute only.
A program may use at most 128 MiB of HBM per device.

```python
import math
import jax
import jax.numpy as jnp
from jax import lax

H = 32
HD = 24
BLOCK = 128
MAXB = 4
D = 768
G = 8
N = 8192
NB = 64


def order_table(key):
    base = jax.random.fold_in(key, 11)
    keys = jax.random.split(base, G)
    return jax.vmap(lambda one: jax.random.permutation(one, N))(keys).astype(jnp.int32)


def draw_grouped_vertex_permutation(key, part):
    return order_table(key)


def draw_vertex_embeddings(key, part):
    order = order_table(key)
    noise_key, offset_key, strength_key = jax.random.split(jax.random.fold_in(key, 23), 3)
    offsets = jax.random.randint(offset_key, (G, NB, 2), 0, BLOCK)
    lane = jnp.arange(BLOCK, dtype=jnp.int32)
    marked = jnp.any(lane[None, None, None, :] == offsets[..., None], axis=2)
    marked = marked.reshape(G, N).astype(jnp.float32)
    placed = jax.vmap(lambda where, flags: jnp.zeros((N,), jnp.float32).at[where].set(flags))(order, marked)
    base = jnp.clip(jax.random.normal(noise_key, (G, N, D), jnp.float32), -2.5, 2.5)
    strength = jnp.exp(jax.random.uniform(strength_key, (G, N), jnp.float32, math.log(1.5), math.log(3.0)))
    drawn = jnp.ones((G, N), jnp.float32)
    score_scale = drawn + placed * (strength - drawn)
    return (base * score_scale[..., None]).astype(jnp.bfloat16)


def draw_listed_tiles(key, part):
    raw = jax.random.randint(key, (G, H, NB, NB), 0, 1 << 20)
    cols = jnp.arange(NB, dtype=jnp.int32)
    score = raw * NB + cols[None, None, None, :]
    own = cols[:, None] == cols[None, :]
    score = jnp.where(own[None, None, :, :], 1 << 30, score)
    picked = lax.top_k(score, MAXB)[1]
    return picked.astype(jnp.int32)


def draw_active_tile_tally(key, part):
    first, second = jax.random.split(key)
    base = jax.random.randint(first, (G, H, NB), 1, MAXB + 1)
    where_full = jax.random.randint(second, (G, H, 1), 0, NB)
    cols = jnp.arange(NB, dtype=jnp.int32)[None, None, :]
    return jnp.where(cols == where_full, MAXB, base).astype(jnp.int32)


def levels(own_key, shape, cuts, least, high):
    loudness, own = 1.0, jax.random.fold_in(own_key, 6)
    for dim, shards_of in cuts:
        steps = jnp.exp(jax.random.uniform(jax.random.fold_in(own, dim), (shards_of,), jnp.float32, least / len(cuts), high / len(cuts)))
        loudness = loudness * jnp.repeat(steps, shape[dim] // shards_of).reshape([-1 if axis == dim else 1 for axis in range(len(shape))])
    return loudness


def noise(rng, dims, deviation, reach, pieces=(), held_as=jnp.bfloat16):
    array = deviation * jax.random.normal(rng, dims, jnp.float32)
    if pieces:
        array = array * levels(rng, dims, pieces, -0.22, 0.18)
    return jnp.clip(array, -reach, reach).astype(held_as)


def setup_inputs(seed: int = 0) -> dict:
    streams_of = jax.random.split(jax.random.key(seed), 10)
    return {
        "vertex_embeddings": draw_vertex_embeddings(jax.random.fold_in(streams_of[9], 71), 0),
        "incoming_adjoint": noise(streams_of[1], (G, N, D), 1.0, 6.0, ((0, 8), (1, 16))),
        "asking_projector_matrix": noise(streams_of[2], (D, D), D ** -0.5, 0.21875),
        "lookup_projector_matrix": noise(streams_of[3], (D, D), D ** -0.5, 0.21875),
        "content_projector_matrix": noise(streams_of[4], (D, D), D ** -0.5, 0.21875),
        "final_projector_matrix": noise(streams_of[5], (D, D), D ** -0.5, 0.21875),
        "grouped_vertex_permutation": draw_grouped_vertex_permutation(jax.random.fold_in(streams_of[9], 71), 0),
        "listed_tiles": draw_listed_tiles(jax.random.fold_in(streams_of[9], 71), 0),
        "active_tile_tally": draw_active_tile_tally(jax.random.fold_in(streams_of[9], 71), 0),
    }


def head_pass(args):
    qh, kh, vh, doh, ids, cnt = args
    block_count, neighbor_slots = ids.shape
    block_slice = qh.shape[0] // block_count
    head_width = qh.shape[1]
    score_scale = 1.0 / math.sqrt(head_width)
    query_block = qh.reshape(block_count, block_slice, head_width).astype(jnp.float32)
    key_gathered = kh.reshape(block_count, block_slice, head_width)[ids].reshape(block_count, neighbor_slots * block_slice, head_width).astype(jnp.float32)
    value_gathered = vh.reshape(block_count, block_slice, head_width)[ids].reshape(block_count, neighbor_slots * block_slice, head_width).astype(jnp.float32)
    output_gradient_block = doh.reshape(block_count, block_slice, head_width).astype(jnp.float32)
    score_block = jnp.einsum('fce,fte->fct', query_block, key_gathered) * score_scale
    live = (jnp.arange(neighbor_slots * block_slice) // block_slice)[None, None, :] < cnt[:, None, None]
    score_block = jnp.where(live, score_block, -1e+30)
    top = lax.optimization_barrier(jnp.max(score_block, axis=-1, keepdims=True))
    expo = jnp.exp(score_block - top)
    prob = expo / lax.optimization_barrier(jnp.sum(expo, axis=-1, keepdims=True))
    probability_block = prob.astype(jnp.bfloat16).astype(jnp.float32)
    output_rows = jnp.einsum('xow,xwv->xov', probability_block, value_gathered).astype(jnp.bfloat16)
    probability_gradient = jnp.einsum('fce,fte->fct', output_gradient_block, value_gathered)
    delta = lax.optimization_barrier(jnp.sum(prob * probability_gradient, axis=-1, keepdims=True))
    score_gradient = (prob * (probability_gradient - delta) * score_scale).astype(jnp.bfloat16).astype(jnp.float32)
    query_gradient = jnp.einsum('xow,xwv->xov', score_gradient, key_gathered)
    key_gradient_gathered = jnp.einsum('wjh,wjs->whs', score_gradient, query_block).reshape(block_count, neighbor_slots, block_slice, head_width)
    value_gradient_gathered = jnp.einsum('wjh,wjs->whs', probability_block, output_gradient_block).reshape(block_count, neighbor_slots, block_slice, head_width)
    dk = jnp.zeros((block_count, block_slice, head_width), jnp.float32).at[ids].add(key_gradient_gathered)
    dv = jnp.zeros((block_count, block_slice, head_width), jnp.float32).at[ids].add(value_gradient_gathered)
    total = block_count * block_slice
    return (output_rows.reshape(total, head_width), query_gradient.reshape(total, head_width), dk.reshape(total, head_width), dv.reshape(total, head_width))

def partition_tiles(asking_projector_matrix, lookup_projector_matrix, content_projector_matrix, final_projector_matrix):

    def run(args):
        xg, dyg, order, ids, cnt = args
        q = jnp.dot(xg, asking_projector_matrix, preferred_element_type=jnp.float32).astype(jnp.bfloat16)
        k = jnp.dot(xg, lookup_projector_matrix, preferred_element_type=jnp.float32).astype(jnp.bfloat16)
        v = jnp.dot(xg, content_projector_matrix, preferred_element_type=jnp.float32).astype(jnp.bfloat16)
        upstream = jnp.dot(dyg, final_projector_matrix.T, preferred_element_type=jnp.float32).astype(jnp.bfloat16)

        def heads_of(a):
            return a[order].reshape(N, H, HD).transpose(1, 0, 2)
        res = lax.map(head_pass, (heads_of(q), heads_of(k), heads_of(v), heads_of(upstream), ids, cnt))

        def restore(a, dtype):
            flat = a.transpose(1, 0, 2).reshape(N, H * HD).astype(dtype)
            return jnp.zeros((N, H * HD), dtype).at[order].set(flat)
        output_rows = restore(res[0], jnp.bfloat16)
        query_gradient = restore(res[1], jnp.bfloat16)
        dk = restore(res[2], jnp.bfloat16)
        dv = restore(res[3], jnp.bfloat16)
        result = jnp.dot(output_rows, final_projector_matrix, preferred_element_type=jnp.float32).astype(jnp.bfloat16)
        back = (jnp.dot(query_gradient, asking_projector_matrix.T, preferred_element_type=jnp.float32) + jnp.dot(dk, lookup_projector_matrix.T, preferred_element_type=jnp.float32) + jnp.dot(dv, content_projector_matrix.T, preferred_element_type=jnp.float32)).astype(jnp.bfloat16)
        derivative_bundle = jnp.stack([jnp.dot(xg.T, query_gradient, preferred_element_type=jnp.float32), jnp.dot(xg.T, dk, preferred_element_type=jnp.float32), jnp.dot(xg.T, dv, preferred_element_type=jnp.float32), jnp.dot(output_rows.T, dyg, preferred_element_type=jnp.float32)])
        return (result, back, derivative_bundle)
    return run

def reference(vertex_embeddings, incoming_adjoint, asking_projector_matrix, lookup_projector_matrix, content_projector_matrix, final_projector_matrix, grouped_vertex_permutation, listed_tiles, active_tile_tally):
    sublayer_yield, embedding_derivative, derivative_bundle = lax.map(partition_tiles(asking_projector_matrix, lookup_projector_matrix, content_projector_matrix, final_projector_matrix), (vertex_embeddings, incoming_adjoint, grouped_vertex_permutation, listed_tiles, active_tile_tally))
    factor = 1.0 / math.sqrt(G * N)
    summed = lax.optimization_barrier(jnp.sum(derivative_bundle, axis=0)) * factor
    return (sublayer_yield, embedding_derivative, summed[0], summed[1], summed[2], summed[3])
```

```python
import functools
import math

import jax
import jax.numpy as jnp
from jax import lax
from jax.experimental import pallas as pl
from jax.experimental.pallas import tpu as pltpu
from jax.sharding import PartitionSpec as P

H = 32
HD = 24
BLOCK = 128
ROW_UNROLL = 16
F32 = jnp.float32
BF16 = jnp.bfloat16
NT = (((1,), (1,)), ((), ()))
NN = (((1,), (0,)), ((), ()))


def dot(a, b, dims):
    return lax.dot_general(a, b, dims, preferred_element_type=F32)


def eye():
    r = lax.broadcasted_iota(jnp.int32, (BLOCK, BLOCK), 0)
    c = lax.broadcasted_iota(jnp.int32, (BLOCK, BLOCK), 1)
    return jnp.where(r == c, 1.0, 0.0).astype(BF16)


def attend_kernel(
    heads,
    nblocks,
    slots,
    per_source,
    order_ref,
    ids_ref,
    count_ref,
    q_ref,
    k_ref,
    v_ref,
    up_ref,
    o_out,
    dq_out,
    dk_out,
    dv_out,
    rows_a,
    rows_b,
    x_rows,
    rhs_score,
    kv_cols,
    oq_cols,
    acc,
    bucket,
    fill,
):
    scale = 1.0 / math.sqrt(HD)
    pad = jnp.zeros((BLOCK - 4 * HD, BLOCK), F32)
    gap = jnp.zeros((HD, BLOCK), F32)
    ident = eye()

    def to_rows(j, _):
        src = j // per_source
        col = pl.multiple_of((j % per_source) * BLOCK, BLOCK)
        parts = [r[src, :, pl.ds(col, BLOCK)].astype(F32) for r in (q_ref, k_ref, v_ref, up_ref)]
        at = pl.multiple_of(j * BLOCK, BLOCK)
        for h in range(heads):
            tall = jnp.concatenate([p[h * HD : (h + 1) * HD] for p in parts] + [pad], axis=0)
            rows_a[h, pl.ds(at, BLOCK), :] = dot(ident, tall.astype(BF16), NT)
        return 0

    lax.fori_loop(0, nblocks, to_rows, 0)

    def fetch(i, _):
        base = pl.multiple_of(i * ROW_UNROLL, ROW_UNROLL)
        for u in range(ROW_UNROLL):
            node = order_ref[base + u]
            for h in range(heads):
                rows_b[h, pl.ds(base + u, 1), :] = rows_a[h, pl.ds(node, 1), :]
        return 0

    lax.fori_loop(0, nblocks * BLOCK // ROW_UNROLL, fetch, 0)

    def forms(j, _):
        at = pl.multiple_of(j * BLOCK, BLOCK)
        for h in range(heads):
            rows = rows_b[h, pl.ds(at, BLOCK), :].astype(BF16)
            x_rows[h, j] = rows
            tall = dot(ident, rows, NT)
            q_t, up_t = tall[0:HD], tall[3 * HD : 4 * HD]
            score = jnp.concatenate([gap, q_t, gap, gap, pad], axis=0).astype(BF16)
            value = jnp.concatenate([gap, gap, up_t, gap, pad], axis=0).astype(BF16)
            rhs_score[h, j] = jnp.concatenate([score, value], axis=1)
            kv_cols[h, j] = tall[HD : 3 * HD].astype(BF16)
            acc[h, j] = jnp.zeros((BLOCK, BLOCK), F32)
        return 0

    lax.fori_loop(0, nblocks, forms, 0)

    for c in range(slots):
        fill[c] = 0

    def place(i, _):
        c = count_ref[i] - 1
        n = fill[c]
        bucket[c * heads * nblocks + n] = i
        fill[c] = n + 1
        return 0

    lax.fori_loop(0, heads * nblocks, place, 0)

    lane = lax.broadcasted_iota(jnp.int32, (BLOCK, BLOCK), 1)
    q_lanes = lane < HD
    up_lanes = (lane >= 3 * HD) & (lane < 4 * HD)

    def attend(items, live):
        where = []
        for i in items:
            h = i // nblocks
            b = i % nblocks
            ids = [ids_ref[i * slots + m] for m in range(live)]
            where.append((h, b, ids))
        both = []
        for h, b, ids in where:
            keys = jnp.concatenate([x_rows[h, j] for j in ids], axis=0)
            both.append(dot(keys, rhs_score[h, b], NN))
        back = []
        for s in both:
            score = s[:, :BLOCK] * scale
            dprob = s[:, BLOCK:]
            top = jnp.max(score, axis=0, keepdims=True)
            expo = jnp.exp(score - top)
            prob = expo * (1.0 / jnp.sum(expo, axis=0, keepdims=True))
            delta = jnp.sum(prob * dprob, axis=0, keepdims=True)
            dscore = prob * (dprob - delta) * scale
            back.append(jnp.concatenate([dscore.astype(BF16), prob.astype(BF16)], axis=1))
        for (h, b, ids), g in zip(where, back):
            cols = jnp.concatenate([kv_cols[h, j] for j in ids], axis=1)
            oq = dot(cols, g, NN)
            oq_cols[h, b] = jnp.concatenate([oq[:HD, :BLOCK], oq[HD:, BLOCK:]], axis=0).astype(BF16)
        grads = []
        for (h, b, ids), g in zip(where, back):
            rows = x_rows[h, b]
            zero = jnp.zeros_like(rows)
            weight = jnp.concatenate(
                [jnp.where(q_lanes, rows, zero), jnp.where(up_lanes, rows, zero)], axis=0
            )
            grads.append(dot(g, weight, NN))
        for (h, b, ids), d in zip(where, grads):
            for m, j in enumerate(ids):
                acc[h, j] += d[m * BLOCK : (m + 1) * BLOCK]

    for c in range(slots):
        base = c * heads * nblocks
        total = fill[c]

        def pair(t, _, c=c, base=base):
            attend([bucket[base + 2 * t], bucket[base + 2 * t + 1]], c + 1)
            return 0

        lax.fori_loop(0, total // 2, pair, 0)

        @pl.when(total % 2 == 1)
        def _(c=c, base=base, total=total):
            attend([bucket[base + total - 1]], c + 1)

    def results(j, _):
        at = pl.multiple_of(j * BLOCK, BLOCK)
        for h in range(heads):
            oq = oq_cols[h, j].astype(F32)
            tall = jnp.concatenate([gap, oq, gap, pad], axis=0).astype(BF16)
            rows_b[h, pl.ds(at, BLOCK), :] = dot(ident, tall, NT) + acc[h, j]
        return 0

    lax.fori_loop(0, nblocks, results, 0)

    def put(i, _):
        base = pl.multiple_of(i * ROW_UNROLL, ROW_UNROLL)
        for u in range(ROW_UNROLL):
            node = order_ref[base + u]
            for h in range(heads):
                rows_a[h, pl.ds(node, 1), :] = rows_b[h, pl.ds(base + u, 1), :]
        return 0

    lax.fori_loop(0, nblocks * BLOCK // ROW_UNROLL, put, 0)

    def to_cols(j, _):
        dst = j // per_source
        col = pl.multiple_of((j % per_source) * BLOCK, BLOCK)
        at = pl.multiple_of(j * BLOCK, BLOCK)
        tall = [dot(ident, rows_a[h, pl.ds(at, BLOCK), :].astype(BF16), NT) for h in range(heads)]
        for slot, out in enumerate((dk_out, dq_out, o_out, dv_out)):
            cut = jnp.concatenate([t[slot * HD : (slot + 1) * HD] for t in tall], axis=0)
            out[dst, :, pl.ds(col, BLOCK)] = cut.astype(BF16)
        return 0

    lax.fori_loop(0, nblocks, to_cols, 0)


def attend_all(order, ids, counts, q, k, v, up, interpret=False):
    sources, feats, width = q.shape
    heads = feats // HD
    total = sources * width
    nblocks = total // BLOCK
    slots = ids.shape[-1]
    items = heads * nblocks
    smem = pl.BlockSpec(memory_space=pltpu.SMEM)
    vmem = pl.BlockSpec(memory_space=pltpu.VMEM)
    out = jax.ShapeDtypeStruct((sources, feats, width), BF16)
    return pl.pallas_call(
        functools.partial(attend_kernel, heads, nblocks, slots, width // BLOCK),
        out_shape=[out] * 4,
        in_specs=[smem] * 3 + [vmem] * 4,
        out_specs=[vmem] * 4,
        scratch_shapes=[
            pltpu.VMEM((heads, total, BLOCK), F32),
            pltpu.VMEM((heads, total, BLOCK), F32),
            pltpu.VMEM((heads, nblocks, BLOCK, BLOCK), BF16),
            pltpu.VMEM((heads, nblocks, BLOCK, 2 * BLOCK), BF16),
            pltpu.VMEM((heads, nblocks, 2 * HD, BLOCK), BF16),
            pltpu.VMEM((heads, nblocks, 2 * HD, BLOCK), BF16),
            pltpu.VMEM((heads, nblocks, BLOCK, BLOCK), F32),
            pltpu.SMEM((slots * items,), jnp.int32),
            pltpu.SMEM((slots,), jnp.int32),
        ],
        compiler_params=pltpu.CompilerParams(vmem_limit_bytes=60000 * 1024),
        interpret=interpret,
        name="attend",
    )(order, ids.reshape(-1), counts.reshape(-1), q, k, v, up)


def project(weight, rows):
    return lax.dot_general(
        weight, rows, (((0,), (1,)), ((), ())), preferred_element_type=jnp.float32
    ).astype(jnp.bfloat16)


def local(
    vertex_embeddings,
    incoming_adjoint,
    asking_projector_matrix,
    lookup_projector_matrix,
    content_projector_matrix,
    final_projector_matrix,
    grouped_vertex_permutation,
    listed_tiles,
    active_tile_tally,
):
    rows = vertex_embeddings[0]
    cotan = incoming_adjoint[0]
    parts = lax.axis_size("node")
    local_heads = H // parts
    feats = local_heads * HD
    width = rows.shape[0]
    total = parts * width
    upstream = lax.dot_general(
        final_projector_matrix, cotan, (((1,), (1,)), ((), ())), preferred_element_type=jnp.float32
    ).astype(jnp.bfloat16)
    sent = [
        project(asking_projector_matrix, rows),
        project(lookup_projector_matrix, rows),
        project(content_projector_matrix, rows),
        upstream,
    ]

    def swap(arr):
        return lax.all_to_all(arr, "node", split_axis=0, concat_axis=0, tiled=True)

    got = [swap(t.reshape(parts, feats, width)) for t in sent]
    first = lax.axis_index("node") * local_heads
    lists = lax.dynamic_slice_in_dim(listed_tiles[0], first, local_heads, 0)
    live_counts = lax.dynamic_slice_in_dim(active_tile_tally[0], first, local_heads, 0)
    done = attend_all(grouped_vertex_permutation[0], lists, live_counts, *got)
    out_nodes, dq, dk, dv = [swap(t).reshape(parts * feats, width) for t in done]
    dims_first = (((0,), (0,)), ((), ()))
    result = lax.dot_general(
        out_nodes, final_projector_matrix, dims_first, preferred_element_type=jnp.float32
    ).astype(jnp.bfloat16)
    dims_back = (((0,), (1,)), ((), ()))
    backward = (
        lax.dot_general(dq, asking_projector_matrix, dims_back, preferred_element_type=jnp.float32)
        + lax.dot_general(dk, lookup_projector_matrix, dims_back, preferred_element_type=jnp.float32)
        + lax.dot_general(dv, content_projector_matrix, dims_back, preferred_element_type=jnp.float32)
    ).astype(jnp.bfloat16)
    dims_weight = (((0,), (1,)), ((), ()))
    stacked = jnp.stack(
        [
            lax.dot_general(rows, dq, dims_weight, preferred_element_type=jnp.float32),
            lax.dot_general(rows, dk, dims_weight, preferred_element_type=jnp.float32),
            lax.dot_general(rows, dv, dims_weight, preferred_element_type=jnp.float32),
            jnp.dot(out_nodes, cotan, preferred_element_type=jnp.float32),
        ]
    )
    summed = lax.psum(stacked, ("dp", "node"))
    factor = 1.0 / math.sqrt(lax.axis_size("dp") * total)
    summed = summed * factor
    return (result[None], backward[None], summed[0], summed[1], summed[2], summed[3])


def solution(mesh):
    placed = (
        P("dp", "node", None),
        P("dp", "node", None),
        P(),
        P(),
        P(),
        P(),
        P("dp", None),
        P("dp", None, None, None),
        P("dp", None, None),
    )
    return jax.shard_map(
        local,
        mesh=mesh,
        in_specs=placed,
        out_specs=(P("dp", "node", None), P("dp", "node", None), P(), P(), P(), P()),
        check_vma=False,
    )
```

```python
import functools
import math

import jax
import jax.numpy as jnp
from jax import lax
from jax.experimental import pallas as pl
from jax.experimental.pallas import tpu as pltpu
from jax.sharding import PartitionSpec as P

H = 32
HD = 24
BLOCK = 128
ROW_UNROLL = 16
F32 = jnp.float32
BF16 = jnp.bfloat16
NT = (((1,), (1,)), ((), ()))
NN = (((1,), (0,)), ((), ()))


def dot(a, b, dims):
    return lax.dot_general(a, b, dims, preferred_element_type=F32)


def eye():
    r = lax.broadcasted_iota(jnp.int32, (BLOCK, BLOCK), 0)
    c = lax.broadcasted_iota(jnp.int32, (BLOCK, BLOCK), 1)
    return jnp.where(r == c, 1.0, 0.0).astype(BF16)


def attend_kernel(
    nblocks,
    slots,
    per_source,
    order_ref,
    ids_ref,
    count_ref,
    in_ref,
    out_ref,
    rows_a,
    rows_b,
    x_rows,
    rhs_score,
    kv_cols,
    oq_cols,
    acc,
    bucket,
    fill,
):
    scale = 1.0 / math.sqrt(HD)
    pad = jnp.zeros((BLOCK - 4 * HD, BLOCK), F32)
    pad_half = jnp.zeros((BLOCK - 4 * HD, BLOCK), BF16)
    gap = jnp.zeros((HD, BLOCK), F32)
    ident = eye()

    def to_rows(j, _):
        src = j // per_source
        col = pl.multiple_of((j % per_source) * BLOCK, BLOCK)
        at = pl.multiple_of(j * BLOCK, BLOCK)
        tall = jnp.concatenate([in_ref[src, :, pl.ds(col, BLOCK)], pad_half], axis=0)
        rows_a[pl.ds(at, BLOCK), :] = dot(ident, tall, NT)
        return 0

    lax.fori_loop(0, nblocks, to_rows, 0, unroll=4)

    def fetch(i, _):
        base = pl.multiple_of(i * ROW_UNROLL, ROW_UNROLL)
        for u in range(ROW_UNROLL):
            rows_b[pl.ds(base + u, 1), :] = rows_a[pl.ds(order_ref[base + u], 1), :]
        return 0

    lax.fori_loop(0, nblocks * BLOCK // ROW_UNROLL, fetch, 0)

    def forms(j, _):
        at = pl.multiple_of(j * BLOCK, BLOCK)
        rows = rows_b[pl.ds(at, BLOCK), :].astype(BF16)
        x_rows[j] = rows
        tall = dot(ident, rows, NT)
        q_t, up_t = tall[0:HD], tall[3 * HD : 4 * HD]
        score = jnp.concatenate([gap, q_t, gap, gap, pad], axis=0).astype(BF16)
        value = jnp.concatenate([gap, gap, up_t, gap, pad], axis=0).astype(BF16)
        rhs_score[j] = jnp.concatenate([score, value], axis=1)
        kv_cols[j] = tall[HD : 3 * HD].astype(BF16)
        acc[j] = jnp.zeros((BLOCK, BLOCK), F32)
        return 0

    lax.fori_loop(0, nblocks, forms, 0, unroll=4)

    for c in range(slots):
        fill[c] = 0

    def place(i, _):
        c = count_ref[i] - 1
        n = fill[c]
        bucket[c * nblocks + n] = i
        fill[c] = n + 1
        return 0

    lax.fori_loop(0, nblocks, place, 0)

    lane = lax.broadcasted_iota(jnp.int32, (BLOCK, BLOCK), 1)
    q_lanes = lane < HD
    up_lanes = (lane >= 3 * HD) & (lane < 4 * HD)

    def attend(items, live):
        where = [(b, [ids_ref[b * slots + m] for m in range(live)]) for b in items]
        both = []
        for b, ids in where:
            keys = jnp.concatenate([x_rows[j] for j in ids], axis=0)
            both.append(dot(keys, rhs_score[b], NN))
        back = []
        for s in both:
            score = s[:, :BLOCK] * scale
            dprob = s[:, BLOCK:]
            top = jnp.max(score, axis=0, keepdims=True)
            expo = jnp.exp(score - top)
            prob = expo * (1.0 / jnp.sum(expo, axis=0, keepdims=True))
            delta = jnp.sum(prob * dprob, axis=0, keepdims=True)
            dscore = prob * (dprob - delta) * scale
            back.append(jnp.concatenate([dscore.astype(BF16), prob.astype(BF16)], axis=1))
        for (b, ids), g in zip(where, back):
            cols = jnp.concatenate([kv_cols[j] for j in ids], axis=1)
            oq = dot(cols, g, NN)
            oq_cols[b] = jnp.concatenate([oq[:HD, :BLOCK], oq[HD:, BLOCK:]], axis=0).astype(BF16)
        grads = []
        for (b, ids), g in zip(where, back):
            rows = x_rows[b]
            zero = jnp.zeros_like(rows)
            weight = jnp.concatenate(
                [jnp.where(q_lanes, rows, zero), jnp.where(up_lanes, rows, zero)], axis=0
            )
            grads.append(dot(g, weight, NN))
        for (b, ids), d in zip(where, grads):
            for m, j in enumerate(ids):
                acc[j] += d[m * BLOCK : (m + 1) * BLOCK]

    for c in range(slots):
        base = c * nblocks
        total = fill[c]

        def pair(t, _, c=c, base=base):
            attend([bucket[base + 2 * t], bucket[base + 2 * t + 1]], c + 1)
            return 0

        lax.fori_loop(0, total // 2, pair, 0)

        @pl.when(total % 2 == 1)
        def _(c=c, base=base, total=total):
            attend([bucket[base + total - 1]], c + 1)

    def results(j, _):
        at = pl.multiple_of(j * BLOCK, BLOCK)
        oq = oq_cols[j].astype(F32)
        tall = jnp.concatenate([gap, oq, gap, pad], axis=0).astype(BF16)
        rows_b[pl.ds(at, BLOCK), :] = dot(ident, tall, NT) + acc[j]
        return 0

    lax.fori_loop(0, nblocks, results, 0, unroll=4)

    def put(i, _):
        base = pl.multiple_of(i * ROW_UNROLL, ROW_UNROLL)
        for u in range(ROW_UNROLL):
            rows_a[pl.ds(order_ref[base + u], 1), :] = rows_b[pl.ds(base + u, 1), :]
        return 0

    lax.fori_loop(0, nblocks * BLOCK // ROW_UNROLL, put, 0)

    def to_cols(j, _):
        dst = j // per_source
        col = pl.multiple_of((j % per_source) * BLOCK, BLOCK)
        at = pl.multiple_of(j * BLOCK, BLOCK)
        tall = dot(ident, rows_a[pl.ds(at, BLOCK), :].astype(BF16), NT)
        out_ref[dst, :, pl.ds(col, BLOCK)] = tall[: 4 * HD].astype(BF16)
        return 0

    lax.fori_loop(0, nblocks, to_cols, 0, unroll=4)


def attend_head(order, ids, counts, arrived):
    sources, feats, width = arrived.shape
    total = sources * width
    nblocks = total // BLOCK
    slots = ids.shape[-1]
    smem = pl.BlockSpec(memory_space=pltpu.SMEM)
    vmem = pl.BlockSpec(memory_space=pltpu.VMEM)
    return pl.pallas_call(
        functools.partial(attend_kernel, nblocks, slots, width // BLOCK),
        out_shape=jax.ShapeDtypeStruct((sources, feats, width), BF16),
        in_specs=[smem] * 3 + [vmem],
        out_specs=vmem,
        scratch_shapes=[
            pltpu.VMEM((total, BLOCK), F32),
            pltpu.VMEM((total, BLOCK), F32),
            pltpu.VMEM((nblocks, BLOCK, BLOCK), BF16),
            pltpu.VMEM((nblocks, BLOCK, 2 * BLOCK), BF16),
            pltpu.VMEM((nblocks, 2 * HD, BLOCK), BF16),
            pltpu.VMEM((nblocks, 2 * HD, BLOCK), BF16),
            pltpu.VMEM((nblocks, BLOCK, BLOCK), F32),
            pltpu.SMEM((slots * nblocks,), jnp.int32),
            pltpu.SMEM((slots,), jnp.int32),
        ],
        compiler_params=pltpu.CompilerParams(vmem_limit_bytes=40000 * 1024),
        cost_estimate=pl.CostEstimate(
            flops=30_000_000_000, bytes_accessed=100_000_000, transcendentals=0
        ),
        name="attend",
    )(order, ids.reshape(-1), counts, arrived)


def project(weight, rows):
    return lax.dot_general(
        weight, rows, (((0,), (1,)), ((), ())), preferred_element_type=jnp.float32
    ).astype(jnp.bfloat16)


def ring(axis_name, size, to_coord, to_index, flip):
    pairs = []
    for i in range(size):
        c = to_coord(i)
        pairs.append((i, to_index(i, 3 - c if flip else c ^ 1)))
    return axis_name, pairs


def torus(dp, node):
    side = 4
    z = lambda i: i // 2
    x = lambda i: i // side
    y = lambda i: i % side
    axes = {
        "z": ("dp", z, lambda i, c: c * 2 + i % 2),
        "x": ("node", x, lambda i, c: c * side + i % side),
        "y": ("node", y, lambda i, c: (i // side) * side + c),
    }
    sizes = {"dp": dp, "node": node}
    out = {}
    for key, (name, coord, index) in axes.items():
        pairings = [ring(name, sizes[name], coord, index, flip) for flip in (False, True)]
        out[key] = (coord(lax.axis_index(name)), pairings)
    return out


def halves_of(arr, cols):
    if cols:
        return arr.reshape(arr.shape[0], 2, arr.shape[1] // 2).transpose(1, 0, 2)
    return arr.reshape(2, arr.shape[0] // 2, arr.shape[1])


def pick(arr, bit):
    return jnp.where(bit == 0, arr[0], arr[1])


def join(mine, other, bit, cols):
    low = jnp.where(bit == 0, mine, other)
    high = jnp.where(bit == 0, other, mine)
    return jnp.concatenate([low, high], axis=1 if cols else 0)


def add(a, b):
    return (a.astype(F32) + b.astype(F32)).astype(BF16)


def all_reduce(grads):
    dp, node = lax.axis_size("dp"), lax.axis_size("node")
    axes = torus(dp, node)
    core = lax.axis_index("dp") % 2
    other_core = [(i, i ^ 1) for i in range(dp)]
    send = [jnp.where(core == 0, grads[2 + i], grads[i]) for i in range(2)]
    keep = [jnp.where(core == 0, grads[i], grads[2 + i]) for i in range(2)]
    part = [add(k, lax.ppermute(s, "dp", other_core)) for k, s in zip(keep, send)]
    plans = []
    for order in ("xyz", "zxy"):
        plan = []
        for key in order:
            coord, pairings = axes[key]
            plan.append((((coord == 1) | (coord == 2)).astype(jnp.int32), pairings[0]))
            plan.append(((coord >= 2).astype(jnp.int32), pairings[1]))
        plans.append(plan)
    steps = len(plans[0])
    for n in range(steps):
        for i in range(2):
            bit, (name, pairs) = plans[i][n]
            two = halves_of(part[i], n == steps - 1)
            got = lax.ppermute(pick(two, 1 - bit), name, pairs)
            part[i] = add(pick(two, bit), got)
    for n in reversed(range(steps)):
        for i in range(2):
            bit, (name, pairs) = plans[i][n]
            part[i] = join(part[i], lax.ppermute(part[i], name, pairs), bit, n == steps - 1)
    got = [lax.ppermute(p, "dp", other_core) for p in part]
    low = [jnp.where(core == 0, p, g) for p, g in zip(part, got)]
    high = [jnp.where(core == 0, g, p) for p, g in zip(part, got)]
    return low + high


def local(
    vertex_embeddings,
    incoming_adjoint,
    asking_projector_matrix,
    lookup_projector_matrix,
    content_projector_matrix,
    final_projector_matrix,
    grouped_vertex_permutation,
    listed_tiles,
    active_tile_tally,
):
    rows = vertex_embeddings[0]
    cotan = incoming_adjoint[0]
    parts = lax.axis_size("node")
    halves = H // parts
    cut = parts * HD
    width = rows.shape[0]
    total = parts * width
    upstream = lax.dot_general(
        final_projector_matrix, cotan, (((1,), (1,)), ((), ())), preferred_element_type=jnp.float32
    ).astype(jnp.bfloat16)
    sent = [
        project(asking_projector_matrix, rows),
        project(lookup_projector_matrix, rows),
        project(content_projector_matrix, rows),
        upstream,
    ]

    def swap(arr):
        return lax.all_to_all(arr, "node", split_axis=0, concat_axis=0, tiled=True)

    me = lax.axis_index("node")
    order = grouped_vertex_permutation[0]
    dims_first = (((0,), (0,)), ((), ()))
    dims_back = (((0,), (1,)), ((), ()))
    back = []
    for n in range(halves):
        part = jnp.stack(
            [t[n * cut : (n + 1) * cut].reshape(parts, HD, width) for t in sent], axis=1
        ).reshape(parts, 4 * HD, width)
        head = n * parts + me
        ids = lax.dynamic_index_in_dim(listed_tiles[0], head, 0, keepdims=False)
        live = lax.dynamic_index_in_dim(active_tile_tally[0], head, 0, keepdims=False)
        done = swap(attend_head(order, ids, live, swap(part))).reshape(parts, 4, HD, width)
        dk, dq, out, dv = [done[:, i].reshape(cut, width) for i in range(4)]
        back.append((dk, dq, out, dv))
    dk, dq, out, dv = [jnp.concatenate(t, axis=0) for t in zip(*back)]
    result = lax.dot_general(
        out, final_projector_matrix, dims_first, preferred_element_type=jnp.float32
    ).astype(jnp.bfloat16)
    backward = (
        lax.dot_general(dq, asking_projector_matrix, dims_back, preferred_element_type=jnp.float32)
        + lax.dot_general(dk, lookup_projector_matrix, dims_back, preferred_element_type=jnp.float32)
        + lax.dot_general(dv, content_projector_matrix, dims_back, preferred_element_type=jnp.float32)
    ).astype(jnp.bfloat16)
    factor = 1.0 / math.sqrt(lax.axis_size("dp") * total)
    grads = [
        lax.dot_general(a, b, dims, preferred_element_type=jnp.float32).astype(jnp.bfloat16)
        for a, b, dims in (
            (dq, rows, NN),
            (dk, rows, NN),
            (dv, rows, NN),
            (out, cotan, NN),
        )
    ]
    summed = all_reduce(grads)
    weights = [(t if i == 3 else t.T).astype(F32) * factor for i, t in enumerate(summed)]
    return (result[None], backward[None], *weights)


def solution(mesh):
    placed = (
        P("dp", "node", None),
        P("dp", "node", None),
        P(),
        P(),
        P(),
        P(),
        P("dp", None),
        P("dp", None, None, None),
        P("dp", None, None),
    )
    return jax.shard_map(
        local,
        mesh=mesh,
        in_specs=placed,
        out_specs=(P("dp", "node", None), P("dp", "node", None), P(), P(), P(), P()),
        check_vma=False,
    )
```

```python
import functools
import math

import jax
import jax.numpy as jnp
from jax import lax
from jax.experimental import pallas as pl
from jax.experimental.pallas import tpu as pltpu
from jax.sharding import PartitionSpec as P

H = 32
HD = 24
BLOCK = 128
ROW_UNROLL = 16
F32 = jnp.float32
BF16 = jnp.bfloat16
NT = (((1,), (1,)), ((), ()))
NN = (((1,), (0,)), ((), ()))


def dot(a, b, dims):
    return lax.dot_general(a, b, dims, preferred_element_type=F32)


def eye():
    r = lax.broadcasted_iota(jnp.int32, (BLOCK, BLOCK), 0)
    c = lax.broadcasted_iota(jnp.int32, (BLOCK, BLOCK), 1)
    return jnp.where(r == c, 1.0, 0.0).astype(BF16)


def attend_kernel(
    nblocks,
    slots,
    per_source,
    order_ref,
    ids_ref,
    count_ref,
    in_ref,
    out_ref,
    rows_a,
    rows_b,
    x_rows,
    rhs_score,
    kv_cols,
    oq_cols,
    acc,
    bucket,
    fill,
):
    scale = 1.0 / math.sqrt(HD)
    pad = jnp.zeros((BLOCK - 4 * HD, BLOCK), F32)
    pad_half = jnp.zeros((BLOCK - 4 * HD, BLOCK), BF16)
    gap = jnp.zeros((HD, BLOCK), F32)
    ident = eye()

    def to_rows(j, _):
        src = j // per_source
        col = pl.multiple_of((j % per_source) * BLOCK, BLOCK)
        at = pl.multiple_of(j * BLOCK, BLOCK)
        tall = jnp.concatenate([in_ref[src, :, pl.ds(col, BLOCK)], pad_half], axis=0)
        rows_a[pl.ds(at, BLOCK), :] = dot(ident, tall, NT)
        return 0

    lax.fori_loop(0, nblocks, to_rows, 0, unroll=4)

    def fetch(i, _):
        base = pl.multiple_of(i * ROW_UNROLL, ROW_UNROLL)
        for u in range(ROW_UNROLL):
            rows_b[pl.ds(base + u, 1), :] = rows_a[pl.ds(order_ref[base + u], 1), :]
        return 0

    lax.fori_loop(0, nblocks * BLOCK // ROW_UNROLL, fetch, 0)

    def forms(j, _):
        at = pl.multiple_of(j * BLOCK, BLOCK)
        rows = rows_b[pl.ds(at, BLOCK), :].astype(BF16)
        x_rows[j] = rows
        tall = dot(ident, rows, NT)
        q_t, up_t = tall[0:HD], tall[3 * HD : 4 * HD]
        score = jnp.concatenate([gap, q_t, gap, gap, pad], axis=0).astype(BF16)
        value = jnp.concatenate([gap, gap, up_t, gap, pad], axis=0).astype(BF16)
        rhs_score[j] = jnp.concatenate([score, value], axis=1)
        kv_cols[j] = tall[HD : 3 * HD].astype(BF16)
        acc[j] = jnp.zeros((BLOCK, BLOCK), F32)
        return 0

    lax.fori_loop(0, nblocks, forms, 0, unroll=4)

    for c in range(slots):
        fill[c] = 0

    def place(i, _):
        c = count_ref[i] - 1
        n = fill[c]
        bucket[c * nblocks + n] = i
        fill[c] = n + 1
        return 0

    lax.fori_loop(0, nblocks, place, 0)

    lane = lax.broadcasted_iota(jnp.int32, (BLOCK, BLOCK), 1)
    q_lanes = lane < HD
    up_lanes = (lane >= 3 * HD) & (lane < 4 * HD)

    def attend(items, live):
        where = [(b, [ids_ref[b * slots + m] for m in range(live)]) for b in items]
        both = []
        for b, ids in where:
            keys = jnp.concatenate([x_rows[j] for j in ids], axis=0)
            both.append(dot(keys, rhs_score[b], NN))
        back = []
        for s in both:
            score = s[:, :BLOCK] * scale
            dprob = s[:, BLOCK:]
            top = jnp.max(score, axis=0, keepdims=True)
            expo = jnp.exp(score - top)
            prob = expo * (1.0 / jnp.sum(expo, axis=0, keepdims=True))
            delta = jnp.sum(prob * dprob, axis=0, keepdims=True)
            dscore = prob * (dprob - delta) * scale
            back.append(jnp.concatenate([dscore.astype(BF16), prob.astype(BF16)], axis=1))
        for (b, ids), g in zip(where, back):
            cols = jnp.concatenate([kv_cols[j] for j in ids], axis=1)
            oq = dot(cols, g, NN)
            oq_cols[b] = jnp.concatenate([oq[:HD, :BLOCK], oq[HD:, BLOCK:]], axis=0).astype(BF16)
        grads = []
        for (b, ids), g in zip(where, back):
            rows = x_rows[b]
            zero = jnp.zeros_like(rows)
            weight = jnp.concatenate(
                [jnp.where(q_lanes, rows, zero), jnp.where(up_lanes, rows, zero)], axis=0
            )
            grads.append(dot(g, weight, NN))
        for (b, ids), d in zip(where, grads):
            for m, j in enumerate(ids):
                acc[j] += d[m * BLOCK : (m + 1) * BLOCK]

    for c in range(slots):
        base = c * nblocks
        total = fill[c]

        def pair(t, _, c=c, base=base):
            attend([bucket[base + 2 * t], bucket[base + 2 * t + 1]], c + 1)
            return 0

        lax.fori_loop(0, total // 2, pair, 0)

        @pl.when(total % 2 == 1)
        def _(c=c, base=base, total=total):
            attend([bucket[base + total - 1]], c + 1)

    def results(j, _):
        at = pl.multiple_of(j * BLOCK, BLOCK)
        oq = oq_cols[j].astype(F32)
        tall = jnp.concatenate([gap, oq, gap, pad], axis=0).astype(BF16)
        rows_b[pl.ds(at, BLOCK), :] = dot(ident, tall, NT) + acc[j]
        return 0

    lax.fori_loop(0, nblocks, results, 0, unroll=4)

    def put(i, _):
        base = pl.multiple_of(i * ROW_UNROLL, ROW_UNROLL)
        for u in range(ROW_UNROLL):
            rows_a[pl.ds(order_ref[base + u], 1), :] = rows_b[pl.ds(base + u, 1), :]
        return 0

    lax.fori_loop(0, nblocks * BLOCK // ROW_UNROLL, put, 0)

    def to_cols(j, _):
        dst = j // per_source
        col = pl.multiple_of((j % per_source) * BLOCK, BLOCK)
        at = pl.multiple_of(j * BLOCK, BLOCK)
        tall = dot(ident, rows_a[pl.ds(at, BLOCK), :].astype(BF16), NT)
        out_ref[dst, :, pl.ds(col, BLOCK)] = tall[: 4 * HD].astype(BF16)
        return 0

    lax.fori_loop(0, nblocks, to_cols, 0, unroll=4)


def attend_head(order, ids, counts, arrived):
    sources, feats, width = arrived.shape
    total = sources * width
    nblocks = total // BLOCK
    slots = ids.shape[-1]
    smem = pl.BlockSpec(memory_space=pltpu.SMEM)
    vmem = pl.BlockSpec(memory_space=pltpu.VMEM)
    return pl.pallas_call(
        functools.partial(attend_kernel, nblocks, slots, width // BLOCK),
        out_shape=jax.ShapeDtypeStruct((sources, feats, width), BF16),
        in_specs=[smem] * 3 + [vmem],
        out_specs=vmem,
        scratch_shapes=[
            pltpu.VMEM((total, BLOCK), F32),
            pltpu.VMEM((total, BLOCK), F32),
            pltpu.VMEM((nblocks, BLOCK, BLOCK), BF16),
            pltpu.VMEM((nblocks, BLOCK, 2 * BLOCK), BF16),
            pltpu.VMEM((nblocks, 2 * HD, BLOCK), BF16),
            pltpu.VMEM((nblocks, 2 * HD, BLOCK), BF16),
            pltpu.VMEM((nblocks, BLOCK, BLOCK), F32),
            pltpu.SMEM((slots * nblocks,), jnp.int32),
            pltpu.SMEM((slots,), jnp.int32),
        ],
        compiler_params=pltpu.CompilerParams(vmem_limit_bytes=40000 * 1024),
        cost_estimate=pl.CostEstimate(
            flops=30_000_000_000, bytes_accessed=100_000_000, transcendentals=0
        ),
        name="attend",
    )(order, ids.reshape(-1), counts, arrived)


def project(weight, rows):
    return lax.dot_general(
        weight, rows, (((0,), (1,)), ((), ())), preferred_element_type=jnp.float32
    ).astype(jnp.bfloat16)


def ring(axis_name, size, to_coord, to_index, flip):
    pairs = []
    for i in range(size):
        c = to_coord(i)
        pairs.append((i, to_index(i, 3 - c if flip else c ^ 1)))
    return axis_name, pairs


def torus(dp, node):
    side = 4
    z = lambda i: i // 2
    x = lambda i: i // side
    y = lambda i: i % side
    axes = {
        "z": ("dp", z, lambda i, c: c * 2 + i % 2),
        "x": ("node", x, lambda i, c: c * side + i % side),
        "y": ("node", y, lambda i, c: (i // side) * side + c),
    }
    sizes = {"dp": dp, "node": node}
    out = {}
    for key, (name, coord, index) in axes.items():
        pairings = [ring(name, sizes[name], coord, index, flip) for flip in (False, True)]
        out[key] = (coord(lax.axis_index(name)), pairings)
    return out


def pick(arr, bit):
    two = arr.reshape(2, arr.shape[0] // 2, arr.shape[1])
    return jnp.where(bit == 0, two[0], two[1])


def join(mine, other, bit):
    low = jnp.where(bit == 0, mine, other)
    high = jnp.where(bit == 0, other, mine)
    return jnp.concatenate([low, high], axis=0)


def add(a, b):
    return (a.astype(F32) + b.astype(F32)).astype(BF16)


def all_reduce(grads, also):
    dp, node = lax.axis_size("dp"), lax.axis_size("node")
    axes = torus(dp, node)
    core = lax.axis_index("dp") % 2
    other_core = [(i, i ^ 1) for i in range(dp)]

    def plan(key):
        coord, pairings = axes[key]
        keep_high = (((coord == 1) | (coord == 2)).astype(jnp.int32), (coord >= 2).astype(jnp.int32))
        return list(zip(keep_high, pairings))

    def swap(arr, step):
        return lax.ppermute(arr, step[1][0], step[1][1])

    def halve(arr, step):
        return pick(arr, step[0]), swap(pick(arr, 1 - step[0]), step)

    send = [jnp.where(core == 0, grads[2 + i], grads[i]) for i in range(2)]
    keep = [jnp.where(core == 0, grads[i], grads[2 + i]) for i in range(2)]
    part = [add(k, lax.ppermute(s, "dp", other_core)) for k, s in zip(keep, send)]
    wide = [plan("x"), plan("z")]
    mid = plan("y")
    for n in range(2):
        pairs = [halve(part[i], wide[i][n]) for i in range(2)]
        if n == 0:
            (kept, got), also = lax.optimization_barrier((pairs[0], also))
            pairs[0] = (kept, got)
        part = [add(kept, got) for kept, got in pairs]
    quarter = part[0].shape[0] // 4
    both = jnp.stack([p.reshape(4, quarter, p.shape[1]) for p in part], axis=1)
    both = both.reshape(8 * quarter, part[0].shape[1])
    for step in mid:
        both = add(*halve(both, step))
    part = [both[:quarter], both[quarter:]]
    for n in range(2):
        part = [add(part[i], swap(part[i], wide[1 - i][n])) for i in range(2)]
    both = jnp.concatenate(part, axis=0)
    for step in reversed(mid):
        both = join(both, swap(both, step), step[0])
    both = both.reshape(4, 2, quarter, both.shape[1])
    part = [both[:, i].reshape(4 * quarter, both.shape[-1]) for i in range(2)]
    for n in reversed(range(2)):
        part = [join(part[i], swap(part[i], wide[i][n]), wide[i][n][0]) for i in range(2)]
    other = [lax.ppermute(p, "dp", other_core) for p in part]
    return core, part, other, also


def finish_kernel(factor, core_ref, q_mine, k_mine, v_mine, o_mine, q_oth, k_oth, v_oth, o_oth, *outs):
    core = core_ref[0]

    def write(q, k, v, o):
        for src, out in zip((q, k, v), outs):
            out[...] = src[...].astype(F32).T * factor
        outs[3][...] = o[...].astype(F32) * factor

    @pl.when(core == 0)
    def _():
        write(q_mine, k_mine, v_oth, o_oth)

    @pl.when(core != 0)
    def _():
        write(q_oth, k_oth, v_mine, o_mine)


def finish(core, part, other, factor):
    size = part[0].shape[0]
    tall = pl.BlockSpec((size, BLOCK), lambda i, c: (0, i))
    wide = pl.BlockSpec((BLOCK, size), lambda i, c: (i, 0))
    specs = [tall, tall, tall, wide]
    args = [part[0], part[1], part[0], part[1], other[0], other[1], other[0], other[1]]
    return pl.pallas_call(
        functools.partial(finish_kernel, factor),
        out_shape=[jax.ShapeDtypeStruct((size, size), F32)] * 4,
        grid_spec=pltpu.PrefetchScalarGridSpec(
            num_scalar_prefetch=1,
            grid=(size // BLOCK,),
            in_specs=specs + specs,
            out_specs=[wide] * 4,
        ),
        name="finish",
    )(core.reshape(1), *args)


def local(
    vertex_embeddings,
    incoming_adjoint,
    asking_projector_matrix,
    lookup_projector_matrix,
    content_projector_matrix,
    final_projector_matrix,
    grouped_vertex_permutation,
    listed_tiles,
    active_tile_tally,
):
    rows = vertex_embeddings[0]
    cotan = incoming_adjoint[0]
    parts = lax.axis_size("node")
    halves = H // parts
    cut = parts * HD
    width = rows.shape[0]
    total = parts * width
    upstream = lax.dot_general(
        final_projector_matrix, cotan, (((1,), (1,)), ((), ())), preferred_element_type=jnp.float32
    ).astype(jnp.bfloat16)
    sent = [
        project(asking_projector_matrix, rows),
        project(lookup_projector_matrix, rows),
        project(content_projector_matrix, rows),
        upstream,
    ]

    def swap(arr):
        return lax.all_to_all(arr, "node", split_axis=0, concat_axis=0, tiled=True)

    me = lax.axis_index("node")
    order = grouped_vertex_permutation[0]
    dims_first = (((0,), (0,)), ((), ()))
    dims_back = (((0,), (1,)), ((), ()))
    back = []
    for n in range(halves):
        part = jnp.stack(
            [t[n * cut : (n + 1) * cut].reshape(parts, HD, width) for t in sent], axis=1
        ).reshape(parts, 4 * HD, width)
        head = n * parts + me
        ids = lax.dynamic_index_in_dim(listed_tiles[0], head, 0, keepdims=False)
        live = lax.dynamic_index_in_dim(active_tile_tally[0], head, 0, keepdims=False)
        done = swap(attend_head(order, ids, live, swap(part))).reshape(parts, 4, HD, width)
        dk, dq, out, dv = [done[:, i].reshape(cut, width) for i in range(4)]
        back.append((dk, dq, out, dv))
    dk, dq, out, dv = [jnp.concatenate(t, axis=0) for t in zip(*back)]
    result = lax.dot_general(
        out, final_projector_matrix, dims_first, preferred_element_type=jnp.float32
    ).astype(jnp.bfloat16)
    backward = (
        lax.dot_general(dq, asking_projector_matrix, dims_back, preferred_element_type=jnp.float32)
        + lax.dot_general(dk, lookup_projector_matrix, dims_back, preferred_element_type=jnp.float32)
        + lax.dot_general(dv, content_projector_matrix, dims_back, preferred_element_type=jnp.float32)
    ).astype(jnp.bfloat16)
    factor = 1.0 / math.sqrt(lax.axis_size("dp") * total)
    grads = [
        lax.dot_general(a, b, dims, preferred_element_type=jnp.float32).astype(jnp.bfloat16)
        for a, b, dims in (
            (dq, rows, NN),
            (dk, rows, NN),
            (dv, rows, NN),
            (out, cotan, NN),
        )
    ]
    core, part, other, (result, backward) = all_reduce(grads, (result, backward))
    weights = finish(core, part, other, factor)
    return (result[None], backward[None], *weights)


def solution(mesh):
    placed = (
        P("dp", "node", None),
        P("dp", "node", None),
        P(),
        P(),
        P(),
        P(),
        P("dp", None),
        P("dp", None, None, None),
        P("dp", None, None),
    )
    return jax.shard_map(
        local,
        mesh=mesh,
        in_specs=placed,
        out_specs=(P("dp", "node", None), P("dp", "node", None), P(), P(), P(), P()),
        check_vma=False,
    )
```

```python
import functools
import math

import jax
import jax.numpy as jnp
from jax import lax
from jax.experimental import pallas as pl
from jax.experimental.pallas import tpu as pltpu
from jax.sharding import PartitionSpec as P

H = 32
HD = 24
BLOCK = 128
ROW_UNROLL = 64
GROUP = 4
LOG2E = math.log2(math.e)
F32 = jnp.float32
BF16 = jnp.bfloat16
NT = (((1,), (1,)), ((), ()))
NN = (((1,), (0,)), ((), ()))


def dot(a, b, dims):
    return lax.dot_general(a, b, dims, preferred_element_type=F32)


def eye():
    r = lax.broadcasted_iota(jnp.int32, (BLOCK, BLOCK), 0)
    c = lax.broadcasted_iota(jnp.int32, (BLOCK, BLOCK), 1)
    return jnp.where(r == c, 1.0, 0.0).astype(BF16)


def attend_kernel(
    nblocks,
    slots,
    per_source,
    order_ref,
    ids_ref,
    count_ref,
    in_ref,
    out_ref,
    rows_a,
    rows_b,
    x_rows,
    rhs_score,
    kv_cols,
    oq_cols,
    acc,
    bucket,
    fill,
):
    scale = 1.0 / math.sqrt(HD)
    pad = jnp.zeros((BLOCK - 4 * HD, BLOCK), F32)
    pad_half = jnp.zeros((BLOCK - 4 * HD, BLOCK), BF16)
    gap = jnp.zeros((HD, BLOCK), F32)
    ident = eye()

    def to_rows(j, _):
        src = j // per_source
        col = pl.multiple_of((j % per_source) * BLOCK, BLOCK)
        at = pl.multiple_of(j * BLOCK, BLOCK)
        tall = jnp.concatenate([in_ref[src, :, pl.ds(col, BLOCK)], pad_half], axis=0)
        rows_a[pl.ds(at, BLOCK), :] = dot(ident, tall, NT)
        return 0

    lax.fori_loop(0, nblocks, to_rows, 0, unroll=4)

    def fetch(i, _):
        base = pl.multiple_of(i * ROW_UNROLL, ROW_UNROLL)
        where = order_ref.at[pl.ds(base, ROW_UNROLL)]
        for u in range(ROW_UNROLL):
            rows_b[pl.ds(base + u, 1), :] = rows_a[pl.ds(where[u], 1), :]
        return 0

    lax.fori_loop(0, nblocks * BLOCK // ROW_UNROLL, fetch, 0)

    def forms(j, _):
        at = pl.multiple_of(j * BLOCK, BLOCK)
        rows = rows_b[pl.ds(at, BLOCK), :].astype(BF16)
        x_rows[j] = rows
        tall = dot(ident, rows, NT)
        q_t, up_t = tall[0:HD], tall[3 * HD : 4 * HD]
        score = jnp.concatenate([gap, q_t, gap, gap, pad], axis=0).astype(BF16)
        value = jnp.concatenate([gap, gap, up_t, gap, pad], axis=0).astype(BF16)
        rhs_score[j] = jnp.concatenate([score, value], axis=1)
        kv_cols[j] = tall[HD : 3 * HD].astype(BF16)
        acc[j] = jnp.zeros((BLOCK, BLOCK), F32)
        return 0

    lax.fori_loop(0, nblocks, forms, 0, unroll=4)

    for c in range(slots):
        fill[c] = 0

    def place(i, _):
        c = count_ref[i] - 1
        n = fill[c]
        bucket[c * nblocks + n] = i
        fill[c] = n + 1
        return 0

    lax.fori_loop(0, nblocks, place, 0)

    lane = lax.broadcasted_iota(jnp.int32, (BLOCK, BLOCK), 1)
    q_lanes = lane < HD
    up_lanes = (lane >= 3 * HD) & (lane < 4 * HD)

    def attend(items, live):
        where = [(b, [ids_ref[b * slots + m] for m in range(live)]) for b in items]
        both = []
        for b, ids in where:
            keys = jnp.concatenate([x_rows[j] for j in ids], axis=0)
            both.append(dot(keys, rhs_score[b], NN))
        back = []
        for s in both:
            score = s[:, :BLOCK]
            dprob = s[:, BLOCK:]
            top = jnp.max(score, axis=0, keepdims=True)
            expo = jnp.exp2((score - top) * (scale * LOG2E))
            prob = expo * (1.0 / jnp.sum(expo, axis=0, keepdims=True))
            delta = jnp.sum(prob * dprob, axis=0, keepdims=True)
            dscore = prob * (dprob - delta) * scale
            back.append(jnp.concatenate([dscore.astype(BF16), prob.astype(BF16)], axis=1))
        for (b, ids), g in zip(where, back):
            cols = jnp.concatenate([kv_cols[j] for j in ids], axis=1)
            oq = dot(cols, g, NN)
            oq_cols[b] = jnp.concatenate([oq[:HD, :BLOCK], oq[HD:, BLOCK:]], axis=0).astype(BF16)
        grads = []
        for (b, ids), g in zip(where, back):
            rows = x_rows[b]
            zero = jnp.zeros_like(rows)
            weight = jnp.concatenate(
                [jnp.where(q_lanes, rows, zero), jnp.where(up_lanes, rows, zero)], axis=0
            )
            grads.append(dot(g, weight, NN))
        for (b, ids), d in zip(where, grads):
            for m, j in enumerate(ids):
                acc[j] += d[m * BLOCK : (m + 1) * BLOCK]

    for c in range(slots):
        base = c * nblocks
        total = fill[c]

        def group(t, _, c=c, base=base):
            attend([bucket[base + GROUP * t + u] for u in range(GROUP)], c + 1)
            return 0

        lax.fori_loop(0, total // GROUP, group, 0)

        def single(t, _, c=c, base=base):
            attend([bucket[base + t]], c + 1)
            return 0

        lax.fori_loop(total // GROUP * GROUP, total, single, 0)

    def results(j, _):
        at = pl.multiple_of(j * BLOCK, BLOCK)
        oq = oq_cols[j].astype(F32)
        tall = jnp.concatenate([gap, oq, gap, pad], axis=0).astype(BF16)
        rows_b[pl.ds(at, BLOCK), :] = dot(ident, tall, NT) + acc[j]
        return 0

    lax.fori_loop(0, nblocks, results, 0, unroll=4)

    def put(i, _):
        base = pl.multiple_of(i * ROW_UNROLL, ROW_UNROLL)
        where = order_ref.at[pl.ds(base, ROW_UNROLL)]
        for u in range(ROW_UNROLL):
            rows_a[pl.ds(where[u], 1), :] = rows_b[pl.ds(base + u, 1), :]
        return 0

    lax.fori_loop(0, nblocks * BLOCK // ROW_UNROLL, put, 0)

    def to_cols(j, _):
        dst = j // per_source
        col = pl.multiple_of((j % per_source) * BLOCK, BLOCK)
        at = pl.multiple_of(j * BLOCK, BLOCK)
        tall = dot(ident, rows_a[pl.ds(at, BLOCK), :].astype(BF16), NT)
        out_ref[dst, :, pl.ds(col, BLOCK)] = tall[: 4 * HD].astype(BF16)
        return 0

    lax.fori_loop(0, nblocks, to_cols, 0, unroll=4)


def attend_head(order, ids, counts, arrived):
    sources, feats, width = arrived.shape
    total = sources * width
    nblocks = total // BLOCK
    slots = ids.shape[-1]
    smem = pl.BlockSpec(memory_space=pltpu.SMEM)
    vmem = pl.BlockSpec(memory_space=pltpu.VMEM)
    return pl.pallas_call(
        functools.partial(attend_kernel, nblocks, slots, width // BLOCK),
        out_shape=jax.ShapeDtypeStruct((sources, feats, width), BF16),
        in_specs=[smem] * 3 + [vmem],
        out_specs=vmem,
        scratch_shapes=[
            pltpu.VMEM((total, BLOCK), F32),
            pltpu.VMEM((total, BLOCK), F32),
            pltpu.VMEM((nblocks, BLOCK, BLOCK), BF16),
            pltpu.VMEM((nblocks, BLOCK, 2 * BLOCK), BF16),
            pltpu.VMEM((nblocks, 2 * HD, BLOCK), BF16),
            pltpu.VMEM((nblocks, 2 * HD, BLOCK), BF16),
            pltpu.VMEM((nblocks, BLOCK, BLOCK), F32),
            pltpu.SMEM((slots * nblocks,), jnp.int32),
            pltpu.SMEM((slots,), jnp.int32),
        ],
        compiler_params=pltpu.CompilerParams(vmem_limit_bytes=40000 * 1024),
        cost_estimate=pl.CostEstimate(
            flops=30_000_000_000, bytes_accessed=100_000_000, transcendentals=0
        ),
        name="attend",
    )(order, ids.reshape(-1), counts, arrived)


def project(weight, rows):
    return lax.dot_general(
        weight, rows, (((0,), (1,)), ((), ())), preferred_element_type=jnp.float32
    ).astype(jnp.bfloat16)


def ring(axis_name, size, to_coord, to_index, flip):
    pairs = []
    for i in range(size):
        c = to_coord(i)
        pairs.append((i, to_index(i, 3 - c if flip else c ^ 1)))
    return axis_name, pairs


def torus(dp, node):
    side = 4
    z = lambda i: i // 2
    x = lambda i: i // side
    y = lambda i: i % side
    axes = {
        "z": ("dp", z, lambda i, c: c * 2 + i % 2),
        "x": ("node", x, lambda i, c: c * side + i % side),
        "y": ("node", y, lambda i, c: (i // side) * side + c),
    }
    sizes = {"dp": dp, "node": node}
    out = {}
    for key, (name, coord, index) in axes.items():
        pairings = [ring(name, sizes[name], coord, index, flip) for flip in (False, True)]
        out[key] = (coord(lax.axis_index(name)), pairings)
    return out


def pick(arr, bit):
    two = arr.reshape(2, arr.shape[0] // 2, arr.shape[1])
    return jnp.where(bit == 0, two[0], two[1])


def join(mine, other, bit):
    low = jnp.where(bit == 0, mine, other)
    high = jnp.where(bit == 0, other, mine)
    return jnp.concatenate([low, high], axis=0)


def add(a, b):
    return (a.astype(F32) + b.astype(F32)).astype(BF16)


def all_reduce(grads, also):
    dp, node = lax.axis_size("dp"), lax.axis_size("node")
    axes = torus(dp, node)
    core = lax.axis_index("dp") % 2
    other_core = [(i, i ^ 1) for i in range(dp)]

    def plan(key):
        coord, pairings = axes[key]
        keep_high = (((coord == 1) | (coord == 2)).astype(jnp.int32), (coord >= 2).astype(jnp.int32))
        return list(zip(keep_high, pairings))

    def swap(arr, step):
        return lax.ppermute(arr, step[1][0], step[1][1])

    def halve(arr, step):
        return pick(arr, step[0]), swap(pick(arr, 1 - step[0]), step)

    send = [jnp.where(core == 0, grads[2 + i], grads[i]) for i in range(2)]
    keep = [jnp.where(core == 0, grads[i], grads[2 + i]) for i in range(2)]
    part = [add(k, lax.ppermute(s, "dp", other_core)) for k, s in zip(keep, send)]
    wide = [plan("x"), plan("z")]
    wide = [p[::-1] if m else p for p in wide for m in range(2)]
    mid = [plan("y"), plan("y")[::-1]]
    deep = part[0].shape[0] // 2
    cols = part[0].shape[1]
    chunks = [p[m * deep : (m + 1) * deep] for p in part for m in range(2)]
    for n in range(2):
        pairs = [halve(c, w[n]) for c, w in zip(chunks, wide)]
        if n == 0:
            pairs[3], also = lax.optimization_barrier((pairs[3], also))
        chunks = [add(*p) for p in pairs]
    quarter = chunks[0].shape[0] // 4
    both = []
    for m in range(2):
        two = [chunks[2 * i + m].reshape(4, quarter, cols) for i in range(2)]
        both.append(jnp.stack(two, axis=1).reshape(8 * quarter, cols))
    for n in range(2):
        both = [add(*halve(b, p[n])) for b, p in zip(both, mid)]
    part = [jnp.concatenate([b[i * quarter : (i + 1) * quarter] for b in both]) for i in range(2)]
    for n in range(2):
        part = [add(part[i], swap(part[i], wide[2 - 2 * i][n])) for i in range(2)]
    both = [
        jnp.concatenate([p[m * quarter : (m + 1) * quarter] for p in part]) for m in range(2)
    ]
    for n in (1, 0):
        both = [join(b, swap(b, p[n]), p[n][0]) for b, p in zip(both, mid)]
    both = [b.reshape(4, 2, quarter, cols) for b in both]
    chunks = [both[m][:, i].reshape(4 * quarter, cols) for i in range(2) for m in range(2)]
    for n in (1, 0):
        chunks = [join(c, swap(c, w[n]), w[n][0]) for c, w in zip(chunks, wide)]
    part = [jnp.concatenate(chunks[2 * i : 2 * i + 2]) for i in range(2)]
    other = [lax.ppermute(p, "dp", other_core) for p in part]
    return core, part, other, also


def finish_kernel(factor, core_ref, q_mine, k_mine, v_mine, o_mine, q_oth, k_oth, v_oth, o_oth, *outs):
    core = core_ref[0]

    def write(q, k, v, o):
        for src, out in zip((q, k, v), outs):
            out[...] = src[...].astype(F32).T * factor
        outs[3][...] = o[...].astype(F32) * factor

    @pl.when(core == 0)
    def _():
        write(q_mine, k_mine, v_oth, o_oth)

    @pl.when(core != 0)
    def _():
        write(q_oth, k_oth, v_mine, o_mine)


def finish(core, part, other, factor):
    size = part[0].shape[0]
    wide = pl.BlockSpec((BLOCK, size), lambda i, c: (i, 0))

    def taken(first, tall):
        def at(i, c):
            row = jnp.where(c[0] == first, i, 0)
            return (0, row) if tall else (row, 0)

        return pl.BlockSpec((size, BLOCK) if tall else (BLOCK, size), at)

    specs = [taken(f, t) for f, t in ((0, 1), (0, 1), (1, 1), (1, 0))]
    specs += [taken(f, t) for f, t in ((1, 1), (1, 1), (0, 1), (0, 0))]
    args = [part[0], part[1], part[0], part[1], other[0], other[1], other[0], other[1]]
    return pl.pallas_call(
        functools.partial(finish_kernel, factor),
        out_shape=[jax.ShapeDtypeStruct((size, size), F32)] * 4,
        grid_spec=pltpu.PrefetchScalarGridSpec(
            num_scalar_prefetch=1,
            grid=(size // BLOCK,),
            in_specs=specs,
            out_specs=[wide] * 4,
        ),
        name="finish",
    )(core.reshape(1), *args)


def local(
    vertex_embeddings,
    incoming_adjoint,
    asking_projector_matrix,
    lookup_projector_matrix,
    content_projector_matrix,
    final_projector_matrix,
    grouped_vertex_permutation,
    listed_tiles,
    active_tile_tally,
):
    rows = vertex_embeddings[0]
    cotan = incoming_adjoint[0]
    parts = lax.axis_size("node")
    halves = H // parts
    cut = parts * HD
    width = rows.shape[0]
    total = parts * width
    upstream = lax.dot_general(
        final_projector_matrix, cotan, (((1,), (1,)), ((), ())), preferred_element_type=jnp.float32
    ).astype(jnp.bfloat16)
    sent = [
        project(asking_projector_matrix, rows),
        project(lookup_projector_matrix, rows),
        project(content_projector_matrix, rows),
        upstream,
    ]

    def swap(arr):
        return lax.all_to_all(arr, "node", split_axis=0, concat_axis=0, tiled=True)

    me = lax.axis_index("node")
    order = grouped_vertex_permutation[0]
    dims_first = (((0,), (0,)), ((), ()))
    dims_back = (((0,), (1,)), ((), ()))
    back = []
    for n in range(halves):
        part = jnp.stack(
            [t[n * cut : (n + 1) * cut].reshape(parts, HD, width) for t in sent], axis=1
        ).reshape(parts, 4 * HD, width)
        head = n * parts + me
        ids = lax.dynamic_index_in_dim(listed_tiles[0], head, 0, keepdims=False)
        live = lax.dynamic_index_in_dim(active_tile_tally[0], head, 0, keepdims=False)
        done = swap(attend_head(order, ids, live, swap(part))).reshape(parts, 4, HD, width)
        dk, dq, out, dv = [done[:, i].reshape(cut, width) for i in range(4)]
        back.append((dk, dq, out, dv))
    dk, dq, out, dv = [jnp.concatenate(t, axis=0) for t in zip(*back)]
    result = lax.dot_general(
        out, final_projector_matrix, dims_first, preferred_element_type=jnp.float32
    ).astype(jnp.bfloat16)
    backward = (
        lax.dot_general(dq, asking_projector_matrix, dims_back, preferred_element_type=jnp.float32)
        + lax.dot_general(dk, lookup_projector_matrix, dims_back, preferred_element_type=jnp.float32)
        + lax.dot_general(dv, content_projector_matrix, dims_back, preferred_element_type=jnp.float32)
    ).astype(jnp.bfloat16)
    factor = 1.0 / math.sqrt(lax.axis_size("dp") * total)
    grads = [
        lax.dot_general(a, b, dims, preferred_element_type=jnp.float32).astype(jnp.bfloat16)
        for a, b, dims in (
            (dq, rows, NN),
            (dk, rows, NN),
            (dv, rows, NN),
            (out, cotan, NN),
        )
    ]
    core, part, other, (result, backward) = all_reduce(grads, (result, backward))
    weights = finish(core, part, other, factor)
    return (result[None], backward[None], *weights)


def solution(mesh):
    placed = (
        P("dp", "node", None),
        P("dp", "node", None),
        P(),
        P(),
        P(),
        P(),
        P("dp", None),
        P("dp", None, None, None),
        P("dp", None, None),
    )
    return jax.shard_map(
        local,
        mesh=mesh,
        in_specs=placed,
        out_specs=(P("dp", "node", None), P("dp", "node", None), P(), P(), P(), P()),
        check_vma=False,
    )
```

```python
import functools
import math

import jax
import jax.numpy as jnp
from jax import lax
from jax.experimental import pallas as pl
from jax.experimental.pallas import tpu as pltpu
from jax.sharding import PartitionSpec as P

H = 32
HD = 24
BLOCK = 128
ROW_UNROLL = 64
GROUP = 4
LOG2E = math.log2(math.e)
F32 = jnp.float32
BF16 = jnp.bfloat16
NT = (((1,), (1,)), ((), ()))
NN = (((1,), (0,)), ((), ()))


def dot(a, b, dims):
    return lax.dot_general(a, b, dims, preferred_element_type=F32)


def eye():
    r = lax.broadcasted_iota(jnp.int32, (BLOCK, BLOCK), 0)
    c = lax.broadcasted_iota(jnp.int32, (BLOCK, BLOCK), 1)
    return jnp.where(r == c, 1.0, 0.0).astype(BF16)


def attend_kernel(
    nblocks,
    slots,
    per_source,
    order_ref,
    ids_ref,
    count_ref,
    in_ref,
    out_ref,
    rows_a,
    rows_b,
    x_rows,
    rhs_score,
    kv_cols,
    oq_cols,
    acc,
    bucket,
    fill,
):
    scale = 1.0 / math.sqrt(HD)
    pad = jnp.zeros((BLOCK - 4 * HD, BLOCK), F32)
    pad_half = jnp.zeros((BLOCK - 4 * HD, BLOCK), BF16)
    gap = jnp.zeros((HD, BLOCK), F32)
    ident = eye()

    def to_rows(j, _):
        src = j // per_source
        col = pl.multiple_of((j % per_source) * BLOCK, BLOCK)
        at = pl.multiple_of(j * BLOCK, BLOCK)
        tall = jnp.concatenate([in_ref[src, :, pl.ds(col, BLOCK)], pad_half], axis=0)
        rows_a[pl.ds(at, BLOCK), :] = tall.astype(F32).T
        return 0

    lax.fori_loop(0, nblocks, to_rows, 0, unroll=16)

    def fetch(i, _):
        base = pl.multiple_of(i * ROW_UNROLL, ROW_UNROLL)
        where = order_ref.at[pl.ds(base, ROW_UNROLL)]
        for u in range(ROW_UNROLL):
            rows_b[pl.ds(base + u, 1), :] = rows_a[pl.ds(where[u], 1), :]
        return 0

    lax.fori_loop(0, nblocks * BLOCK // ROW_UNROLL, fetch, 0)

    def forms(j, _):
        at = pl.multiple_of(j * BLOCK, BLOCK)
        rows = rows_b[pl.ds(at, BLOCK), :]
        x_rows[j] = rows.astype(BF16)
        tall = rows.T
        q_t, up_t = tall[0:HD], tall[3 * HD : 4 * HD]
        score = jnp.concatenate([gap, q_t, gap, gap, pad], axis=0).astype(BF16)
        value = jnp.concatenate([gap, gap, up_t, gap, pad], axis=0).astype(BF16)
        rhs_score[j] = jnp.concatenate([score, value], axis=1)
        kv_cols[j] = tall[HD : 3 * HD].astype(BF16)
        acc[j] = jnp.zeros((BLOCK, BLOCK), F32)
        return 0

    lax.fori_loop(0, nblocks, forms, 0, unroll=16)

    for c in range(slots):
        fill[c] = 0

    def place(i, _):
        c = count_ref[i] - 1
        n = fill[c]
        bucket[c * nblocks + n] = i
        fill[c] = n + 1
        return 0

    lax.fori_loop(0, nblocks, place, 0)

    lane = lax.broadcasted_iota(jnp.int32, (BLOCK, BLOCK), 1)
    q_lanes = lane < HD
    up_lanes = (lane >= 3 * HD) & (lane < 4 * HD)

    def attend(items, live):
        where = [(b, [ids_ref[b * slots + m] for m in range(live)]) for b in items]
        both = []
        for b, ids in where:
            keys = jnp.concatenate([x_rows[j] for j in ids], axis=0)
            both.append(dot(keys, rhs_score[b], NN))
        back = []
        for s in both:
            score = s[:, :BLOCK]
            dprob = s[:, BLOCK:]
            top = jnp.max(score, axis=0, keepdims=True)
            expo = jnp.exp2((score - top) * (scale * LOG2E))
            prob = expo * (1.0 / jnp.sum(expo, axis=0, keepdims=True))
            delta = jnp.sum(prob * dprob, axis=0, keepdims=True)
            dscore = prob * (dprob - delta) * scale
            back.append(jnp.concatenate([dscore.astype(BF16), prob.astype(BF16)], axis=1))
        for (b, ids), g in zip(where, back):
            cols = jnp.concatenate([kv_cols[j] for j in ids], axis=1)
            oq = dot(cols, g, NN)
            oq_cols[b] = jnp.concatenate([oq[:HD, :BLOCK], oq[HD:, BLOCK:]], axis=0).astype(BF16)
        grads = []
        for (b, ids), g in zip(where, back):
            rows = x_rows[b]
            zero = jnp.zeros_like(rows)
            weight = jnp.concatenate(
                [jnp.where(q_lanes, rows, zero), jnp.where(up_lanes, rows, zero)], axis=0
            )
            grads.append(dot(g, weight, NN))
        for (b, ids), d in zip(where, grads):
            for m, j in enumerate(ids):
                acc[j] += d[m * BLOCK : (m + 1) * BLOCK]

    for c in range(slots):
        base = c * nblocks
        total = fill[c]

        def group(t, _, c=c, base=base):
            attend([bucket[base + GROUP * t + u] for u in range(GROUP)], c + 1)
            return 0

        lax.fori_loop(0, total // GROUP, group, 0)

        def single(t, _, c=c, base=base):
            attend([bucket[base + t]], c + 1)
            return 0

        lax.fori_loop(total // GROUP * GROUP, total, single, 0)

    def results(j, _):
        at = pl.multiple_of(j * BLOCK, BLOCK)
        oq = oq_cols[j].astype(F32)
        tall = jnp.concatenate([gap, oq, gap, pad], axis=0).astype(BF16)
        rows_b[pl.ds(at, BLOCK), :] = tall.astype(F32).T + acc[j]
        return 0

    lax.fori_loop(0, nblocks, results, 0, unroll=16)

    def put(i, _):
        base = pl.multiple_of(i * ROW_UNROLL, ROW_UNROLL)
        where = order_ref.at[pl.ds(base, ROW_UNROLL)]
        for u in range(ROW_UNROLL):
            rows_a[pl.ds(where[u], 1), :] = rows_b[pl.ds(base + u, 1), :]
        return 0

    lax.fori_loop(0, nblocks * BLOCK // ROW_UNROLL, put, 0)

    def to_cols(j, _):
        dst = j // per_source
        col = pl.multiple_of((j % per_source) * BLOCK, BLOCK)
        at = pl.multiple_of(j * BLOCK, BLOCK)
        tall = rows_a[pl.ds(at, BLOCK), :].T
        out_ref[dst, :, pl.ds(col, BLOCK)] = tall[: 4 * HD].astype(BF16)
        return 0

    lax.fori_loop(0, nblocks, to_cols, 0, unroll=16)


def attend_head(order, ids, counts, arrived):
    sources, feats, width = arrived.shape
    total = sources * width
    nblocks = total // BLOCK
    slots = ids.shape[-1]
    smem = pl.BlockSpec(memory_space=pltpu.SMEM)
    vmem = pl.BlockSpec(memory_space=pltpu.VMEM)
    return pl.pallas_call(
        functools.partial(attend_kernel, nblocks, slots, width // BLOCK),
        out_shape=jax.ShapeDtypeStruct((sources, feats, width), BF16),
        in_specs=[smem] * 3 + [vmem],
        out_specs=vmem,
        scratch_shapes=[
            pltpu.VMEM((total, BLOCK), F32),
            pltpu.VMEM((total, BLOCK), F32),
            pltpu.VMEM((nblocks, BLOCK, BLOCK), BF16),
            pltpu.VMEM((nblocks, BLOCK, 2 * BLOCK), BF16),
            pltpu.VMEM((nblocks, 2 * HD, BLOCK), BF16),
            pltpu.VMEM((nblocks, 2 * HD, BLOCK), BF16),
            pltpu.VMEM((nblocks, BLOCK, BLOCK), F32),
            pltpu.SMEM((slots * nblocks,), jnp.int32),
            pltpu.SMEM((slots,), jnp.int32),
        ],
        compiler_params=pltpu.CompilerParams(vmem_limit_bytes=40000 * 1024),
        cost_estimate=pl.CostEstimate(
            flops=30_000_000_000, bytes_accessed=100_000_000, transcendentals=0
        ),
        name="attend",
    )(order, ids.reshape(-1), counts, arrived)


def project(weight, rows):
    return lax.dot_general(
        weight, rows, (((0,), (1,)), ((), ())), preferred_element_type=jnp.float32
    ).astype(jnp.bfloat16)


def ring(axis_name, size, to_coord, to_index, flip):
    pairs = []
    for i in range(size):
        c = to_coord(i)
        pairs.append((i, to_index(i, 3 - c if flip else c ^ 1)))
    return axis_name, pairs


def torus(dp, node):
    side = 4
    z = lambda i: i // 2
    x = lambda i: i // side
    y = lambda i: i % side
    axes = {
        "z": ("dp", z, lambda i, c: c * 2 + i % 2),
        "x": ("node", x, lambda i, c: c * side + i % side),
        "y": ("node", y, lambda i, c: (i // side) * side + c),
    }
    sizes = {"dp": dp, "node": node}
    out = {}
    for key, (name, coord, index) in axes.items():
        pairings = [ring(name, sizes[name], coord, index, flip) for flip in (False, True)]
        out[key] = (coord(lax.axis_index(name)), pairings)
    return out


def pick(arr, bit):
    two = arr.reshape(2, arr.shape[0] // 2, arr.shape[1])
    return jnp.where(bit == 0, two[0], two[1])


def join(mine, other, bit):
    low = jnp.where(bit == 0, mine, other)
    high = jnp.where(bit == 0, other, mine)
    return jnp.concatenate([low, high], axis=0)


def add(a, b):
    return (a.astype(F32) + b.astype(F32)).astype(BF16)


def all_reduce(grads, also):
    dp, node = lax.axis_size("dp"), lax.axis_size("node")
    axes = torus(dp, node)
    core = lax.axis_index("dp") % 2
    other_core = [(i, i ^ 1) for i in range(dp)]

    def plan(key):
        coord, pairings = axes[key]
        keep_high = (((coord == 1) | (coord == 2)).astype(jnp.int32), (coord >= 2).astype(jnp.int32))
        return list(zip(keep_high, pairings))

    def swap(arr, step):
        return lax.ppermute(arr, step[1][0], step[1][1])

    def halve(arr, step):
        return pick(arr, step[0]), swap(pick(arr, 1 - step[0]), step)

    send = [jnp.where(core == 0, grads[2 + i], grads[i]) for i in range(2)]
    keep = [jnp.where(core == 0, grads[i], grads[2 + i]) for i in range(2)]
    part = [add(k, lax.ppermute(s, "dp", other_core)) for k, s in zip(keep, send)]
    wide = [plan("x"), plan("z")]
    wide = [p[::-1] if m else p for p in wide for m in range(2)]
    mid = plan("y")
    deep = part[0].shape[0] // 2
    cols = part[0].shape[1]
    chunks = [p[m * deep : (m + 1) * deep] for p in part for m in range(2)]
    for n in range(2):
        pairs = [halve(c, w[n]) for c, w in zip(chunks, wide)]
        if n == 0:
            pairs[3], also = lax.optimization_barrier((pairs[3], also))
        chunks = [add(*p) for p in pairs]
    quarter = chunks[0].shape[0] // 4
    both = jnp.stack([c.reshape(4, quarter, cols) for c in chunks], axis=1)
    both = both.reshape(16 * quarter, cols)
    for step in mid:
        both = add(*halve(both, step))
    part = [both[: 2 * quarter], both[2 * quarter :]]
    for n in range(2):
        part = [add(part[i], swap(part[i], wide[2 - 2 * i][n])) for i in range(2)]
    both = jnp.concatenate(part)
    for step in reversed(mid):
        both = join(both, swap(both, step), step[0])
    both = both.reshape(4, 4, quarter, cols)
    chunks = [both[:, k].reshape(4 * quarter, cols) for k in range(4)]
    for n in (1, 0):
        chunks = [join(c, swap(c, w[n]), w[n][0]) for c, w in zip(chunks, wide)]
    part = [jnp.concatenate(chunks[2 * i : 2 * i + 2]) for i in range(2)]
    other = [lax.ppermute(p, "dp", other_core) for p in part]
    return core, part, other, also


def finish_kernel(factor, core_ref, q_mine, k_mine, v_mine, o_mine, q_oth, k_oth, v_oth, o_oth, *outs):
    core = core_ref[0]

    def write(q, k, v, o):
        for src, out in zip((q, k, v), outs):
            out[...] = src[...].astype(F32).T * factor
        outs[3][...] = o[...].astype(F32) * factor

    @pl.when(core == 0)
    def _():
        write(q_mine, k_mine, v_oth, o_oth)

    @pl.when(core != 0)
    def _():
        write(q_oth, k_oth, v_mine, o_mine)


def finish(core, part, other, factor):
    size = part[0].shape[0]
    wide = pl.BlockSpec((BLOCK, size), lambda i, c: (i, 0))

    def taken(first, tall):
        def at(i, c):
            row = jnp.where(c[0] == first, i, 0)
            return (0, row) if tall else (row, 0)

        return pl.BlockSpec((size, BLOCK) if tall else (BLOCK, size), at)

    specs = [taken(f, t) for f, t in ((0, 1), (0, 1), (1, 1), (1, 0))]
    specs += [taken(f, t) for f, t in ((1, 1), (1, 1), (0, 1), (0, 0))]
    args = [part[0], part[1], part[0], part[1], other[0], other[1], other[0], other[1]]
    return pl.pallas_call(
        functools.partial(finish_kernel, factor),
        out_shape=[jax.ShapeDtypeStruct((size, size), F32)] * 4,
        grid_spec=pltpu.PrefetchScalarGridSpec(
            num_scalar_prefetch=1,
            grid=(size // BLOCK,),
            in_specs=specs,
            out_specs=[wide] * 4,
        ),
        name="finish",
    )(core.reshape(1), *args)


def local(
    vertex_embeddings,
    incoming_adjoint,
    asking_projector_matrix,
    lookup_projector_matrix,
    content_projector_matrix,
    final_projector_matrix,
    grouped_vertex_permutation,
    listed_tiles,
    active_tile_tally,
):
    rows = vertex_embeddings[0]
    cotan = incoming_adjoint[0]
    parts = lax.axis_size("node")
    halves = H // parts
    cut = parts * HD
    width = rows.shape[0]
    total = parts * width
    def swap(arr):
        return lax.all_to_all(arr, "node", split_axis=0, concat_axis=0, tiled=True)

    me = lax.axis_index("node")
    order = grouped_vertex_permutation[0]
    dims_first = (((0,), (0,)), ((), ()))
    dims_back = (((0,), (1,)), ((), ()))
    back = []
    for n in range(halves):
        own = slice(n * cut, (n + 1) * cut)
        sent = [
            project(asking_projector_matrix[:, own], rows),
            project(lookup_projector_matrix[:, own], rows),
            project(content_projector_matrix[:, own], rows),
            dot(final_projector_matrix[own], cotan, NT).astype(BF16),
        ]
        part = jnp.stack([t.reshape(parts, HD, width) for t in sent], axis=1)
        part = part.reshape(parts, 4 * HD, width)
        head = n * parts + me
        ids = lax.dynamic_index_in_dim(listed_tiles[0], head, 0, keepdims=False)
        live = lax.dynamic_index_in_dim(active_tile_tally[0], head, 0, keepdims=False)
        done = swap(attend_head(order, ids, live, swap(part))).reshape(parts, 4, HD, width)
        dk, dq, out, dv = [done[:, i].reshape(cut, width) for i in range(4)]
        back.append((dk, dq, out, dv))
    dk, dq, out, dv = [jnp.concatenate(t, axis=0) for t in zip(*back)]
    result = lax.dot_general(
        out, final_projector_matrix, dims_first, preferred_element_type=jnp.float32
    ).astype(jnp.bfloat16)
    backward = (
        lax.dot_general(dq, asking_projector_matrix, dims_back, preferred_element_type=jnp.float32)
        + lax.dot_general(dk, lookup_projector_matrix, dims_back, preferred_element_type=jnp.float32)
        + lax.dot_general(dv, content_projector_matrix, dims_back, preferred_element_type=jnp.float32)
    ).astype(jnp.bfloat16)
    factor = 1.0 / math.sqrt(lax.axis_size("dp") * total)
    grads = [
        lax.dot_general(a, b, dims, preferred_element_type=jnp.float32).astype(jnp.bfloat16)
        for a, b, dims in (
            (dq, rows, NN),
            (dk, rows, NN),
            (dv, rows, NN),
            (out, cotan, NN),
        )
    ]
    core, part, other, (result, backward) = all_reduce(grads, (result, backward))
    weights = finish(core, part, other, factor)
    return (result[None], backward[None], *weights)


def solution(mesh):
    placed = (
        P("dp", "node", None),
        P("dp", "node", None),
        P(),
        P(),
        P(),
        P(),
        P("dp", None),
        P("dp", None, None, None),
        P("dp", None, None),
    )
    return jax.shard_map(
        local,
        mesh=mesh,
        in_specs=placed,
        out_specs=(P("dp", "node", None), P("dp", "node", None), P(), P(), P(), P()),
        check_vma=False,
    )
```

```python
import functools
import math

import jax
import jax.numpy as jnp
from jax import lax
from jax.experimental import pallas as pl
from jax.experimental.pallas import tpu as pltpu
from jax.sharding import PartitionSpec as P


H = 32
HD = 24
BLOCK = 128
ROW_UNROLL = 64
GROUP = (4, 4, 4, 3)
LOG2E = math.log2(math.e)
F32 = jnp.float32
BF16 = jnp.bfloat16
NT = (((1,), (1,)), ((), ()))
NN = (((1,), (0,)), ((), ()))


def dot(a, b, dims):
    return lax.dot_general(a, b, dims, preferred_element_type=F32)


def eye():
    r = lax.broadcasted_iota(jnp.int32, (BLOCK, BLOCK), 0)
    c = lax.broadcasted_iota(jnp.int32, (BLOCK, BLOCK), 1)
    return jnp.where(r == c, 1.0, 0.0).astype(BF16)


def attend_kernel(
    nblocks,
    slots,
    per_source,
    order_ref,
    ids_ref,
    count_ref,
    in_ref,
    out_ref,
    rows_a,
    rows_b,
    x_rows,
    rhs_score,
    kv_cols,
    oq_cols,
    acc,
    bucket,
    fill,
):
    scale = 1.0 / math.sqrt(HD)
    pad = jnp.zeros((BLOCK - 4 * HD, BLOCK), F32)
    pad_half = jnp.zeros((BLOCK - 4 * HD, BLOCK), BF16)
    gap = jnp.zeros((HD, BLOCK), F32)
    ident = eye()

    def to_rows(j, _):
        src = j // per_source
        col = pl.multiple_of((j % per_source) * BLOCK, BLOCK)
        at = pl.multiple_of(j * BLOCK, BLOCK)
        tall = jnp.concatenate([in_ref[src, :, pl.ds(col, BLOCK)], pad_half], axis=0)
        rows_a[pl.ds(at, BLOCK), :] = tall.astype(F32).T
        return 0

    lax.fori_loop(0, nblocks, to_rows, 0, unroll=8)

    def fetch(i, _):
        base = pl.multiple_of(i * ROW_UNROLL, ROW_UNROLL)
        where = order_ref.at[pl.ds(base, ROW_UNROLL)]
        for u in range(ROW_UNROLL):
            rows_b[pl.ds(base + u, 1), :] = rows_a[pl.ds(where[u], 1), :]
        return 0

    lax.fori_loop(0, nblocks * BLOCK // ROW_UNROLL, fetch, 0)

    def forms(j, _):
        at = pl.multiple_of(j * BLOCK, BLOCK)
        rows = rows_b[pl.ds(at, BLOCK), :]
        x_rows[j] = rows.astype(BF16)
        tall = rows.T
        q_t, up_t = tall[0:HD], tall[3 * HD : 4 * HD]
        score = jnp.concatenate([gap, q_t, gap, gap, pad], axis=0).astype(BF16)
        value = jnp.concatenate([gap, gap, up_t, gap, pad], axis=0).astype(BF16)
        rhs_score[j] = jnp.concatenate([score, value], axis=1)
        kv_cols[j] = tall[HD : 3 * HD].astype(BF16)
        acc[j] = jnp.zeros((BLOCK, BLOCK), F32)
        return 0

    lax.fori_loop(0, nblocks, forms, 0, unroll=8)

    for c in range(slots):
        fill[c] = 0

    def place(i, _):
        c = count_ref[i] - 1
        n = fill[c]
        bucket[c * nblocks + n] = i
        fill[c] = n + 1
        return 0

    lax.fori_loop(0, nblocks, place, 0)

    lane = lax.broadcasted_iota(jnp.int32, (BLOCK, BLOCK), 1)
    q_lanes = lane < HD
    up_lanes = (lane >= 3 * HD) & (lane < 4 * HD)

    def attend(items, live):
        where = [(b, [ids_ref[b * slots + m] for m in range(live)]) for b in items]
        both = []
        for b, ids in where:
            keys = jnp.concatenate([x_rows[j] for j in ids], axis=0)
            both.append(dot(keys, rhs_score[b], NN))
        back = []
        for s in both:
            score = s[:, :BLOCK]
            dprob = s[:, BLOCK:]
            top = jnp.max(score, axis=0, keepdims=True)
            expo = jnp.exp2((score - top) * (scale * LOG2E))
            prob = expo * (1.0 / jnp.sum(expo, axis=0, keepdims=True))
            delta = jnp.sum(prob * dprob, axis=0, keepdims=True)
            dscore = prob * (dprob - delta) * scale
            back.append(jnp.concatenate([dscore.astype(BF16), prob.astype(BF16)], axis=1))
        for (b, ids), g in zip(where, back):
            cols = jnp.concatenate([kv_cols[j] for j in ids], axis=1)
            oq = dot(cols, g, NN)
            oq_cols[b] = jnp.concatenate([oq[:HD, :BLOCK], oq[HD:, BLOCK:]], axis=0).astype(BF16)
        grads = []
        for (b, ids), g in zip(where, back):
            rows = x_rows[b]
            zero = jnp.zeros_like(rows)
            weight = jnp.concatenate(
                [jnp.where(q_lanes, rows, zero), jnp.where(up_lanes, rows, zero)], axis=0
            )
            grads.append(dot(g, weight, NN))
        for (b, ids), d in zip(where, grads):
            for m, j in enumerate(ids):
                acc[j] += d[m * BLOCK : (m + 1) * BLOCK]

    for c in range(slots):
        base = c * nblocks
        total = fill[c]

        def group(t, _, c=c, base=base):
            attend([bucket[base + GROUP[c] * t + u] for u in range(GROUP[c])], c + 1)
            return 0

        lax.fori_loop(0, total // GROUP[c], group, 0)

        def single(t, _, c=c, base=base):
            attend([bucket[base + t]], c + 1)
            return 0

        lax.fori_loop(total // GROUP[c] * GROUP[c], total, single, 0)

    def results(j, _):
        at = pl.multiple_of(j * BLOCK, BLOCK)
        oq = oq_cols[j].astype(F32)
        tall = jnp.concatenate([gap, oq, gap, pad], axis=0).astype(BF16)
        rows_b[pl.ds(at, BLOCK), :] = tall.astype(F32).T + acc[j]
        return 0

    lax.fori_loop(0, nblocks, results, 0, unroll=8)

    def put(i, _):
        base = pl.multiple_of(i * ROW_UNROLL, ROW_UNROLL)
        where = order_ref.at[pl.ds(base, ROW_UNROLL)]
        for u in range(ROW_UNROLL):
            rows_a[pl.ds(where[u], 1), :] = rows_b[pl.ds(base + u, 1), :]
        return 0

    lax.fori_loop(0, nblocks * BLOCK // ROW_UNROLL, put, 0)

    def to_cols(j, _):
        dst = j // per_source
        col = pl.multiple_of((j % per_source) * BLOCK, BLOCK)
        at = pl.multiple_of(j * BLOCK, BLOCK)
        tall = rows_a[pl.ds(at, BLOCK), :].T
        out_ref[dst, :, pl.ds(col, BLOCK)] = tall[: 4 * HD].astype(BF16)
        return 0

    lax.fori_loop(0, nblocks, to_cols, 0, unroll=8)


def attend_head(order, ids, counts, arrived):
    sources, feats, width = arrived.shape
    total = sources * width
    nblocks = total // BLOCK
    slots = ids.shape[-1]
    smem = pl.BlockSpec(memory_space=pltpu.SMEM)
    vmem = pl.BlockSpec(memory_space=pltpu.VMEM)
    return pl.pallas_call(
        functools.partial(attend_kernel, nblocks, slots, width // BLOCK),
        out_shape=jax.ShapeDtypeStruct((sources, feats, width), BF16),
        in_specs=[smem] * 3 + [vmem],
        out_specs=vmem,
        scratch_shapes=[
            pltpu.VMEM((total, BLOCK), F32),
            pltpu.VMEM((total, BLOCK), F32),
            pltpu.VMEM((nblocks, BLOCK, BLOCK), BF16),
            pltpu.VMEM((nblocks, BLOCK, 2 * BLOCK), BF16),
            pltpu.VMEM((nblocks, 2 * HD, BLOCK), BF16),
            pltpu.VMEM((nblocks, 2 * HD, BLOCK), BF16),
            pltpu.VMEM((nblocks, BLOCK, BLOCK), F32),
            pltpu.SMEM((slots * nblocks,), jnp.int32),
            pltpu.SMEM((slots,), jnp.int32),
        ],
        compiler_params=pltpu.CompilerParams(vmem_limit_bytes=40000 * 1024),
        cost_estimate=pl.CostEstimate(
            flops=30_000_000_000, bytes_accessed=100_000_000, transcendentals=0
        ),
        name="attend",
    )(order, ids.reshape(-1), counts, arrived)


def project(weight, rows):
    return lax.dot_general(
        weight, rows, (((0,), (1,)), ((), ())), preferred_element_type=jnp.float32
    ).astype(jnp.bfloat16)


def ring(axis_name, size, to_coord, to_index, flip):
    pairs = []
    for i in range(size):
        c = to_coord(i)
        pairs.append((i, to_index(i, 3 - c if flip else c ^ 1)))
    return axis_name, pairs


def torus(dp, node):
    side = 4
    z = lambda i: i // 2
    x = lambda i: i // side
    y = lambda i: i % side
    axes = {
        "z": ("dp", z, lambda i, c: c * 2 + i % 2),
        "x": ("node", x, lambda i, c: c * side + i % side),
        "y": ("node", y, lambda i, c: (i // side) * side + c),
    }
    sizes = {"dp": dp, "node": node}
    out = {}
    for key, (name, coord, index) in axes.items():
        pairings = [ring(name, sizes[name], coord, index, flip) for flip in (False, True)]
        out[key] = (coord(lax.axis_index(name)), pairings)
    return out


def pick(arr, bit):
    two = arr.reshape(2, arr.shape[0] // 2, arr.shape[1])
    return jnp.where(bit == 0, two[0], two[1])


def join(mine, other, bit):
    low = jnp.where(bit == 0, mine, other)
    high = jnp.where(bit == 0, other, mine)
    return jnp.concatenate([low, high], axis=0)


def add(a, b):
    return (a.astype(F32) + b.astype(F32)).astype(BF16)


class Sum:
    def __init__(self):
        self.dp, node = lax.axis_size("dp"), lax.axis_size("node")
        axes = torus(self.dp, node)
        self.core = lax.axis_index("dp") % 2
        self.other_core = [(i, i ^ 1) for i in range(self.dp)]

        def plan(key):
            coord, pairings = axes[key]
            low = ((coord == 1) | (coord == 2)).astype(jnp.int32)
            return list(zip((low, (coord >= 2).astype(jnp.int32)), pairings))

        wide = [plan("z"), plan("x")]
        self.wide = [p[::-1] if m else p for p in wide for m in range(2)]
        self.mid = plan("y")

    def swap(self, arr, step):
        return lax.ppermute(arr, step[1][0], step[1][1])

    def halve(self, arr, step):
        return pick(arr, step[0]), self.swap(pick(arr, 1 - step[0]), step)

    def start(self, head, grads, also=None):
        low, high = [jnp.concatenate(grads[i : i + 2]) for i in (0, 2)]
        send = jnp.where(self.core == 0, high, low)
        keep = jnp.where(self.core == 0, low, high)
        total = add(keep, lax.ppermute(send, "dp", self.other_core))
        deep = total.shape[0] // 2
        chunks = [total[:deep], total[deep:]]
        wide = self.wide[2 * head : 2 * head + 2]
        for n in range(2):
            pairs = [self.halve(c, w[n]) for c, w in zip(chunks, wide)]
            if n == 0 and also is not None:
                pairs[1], also = lax.optimization_barrier((pairs[1], also))
            chunks = [add(*p) for p in pairs]
        return chunks, also

    def end(self, chunks):
        cols = chunks[0].shape[1]
        quarter = chunks[0].shape[0] // 4
        both = jnp.stack([c.reshape(4, quarter, cols) for c in chunks], axis=1)
        both = both.reshape(16 * quarter, cols)
        for step in self.mid:
            both = add(*self.halve(both, step))
        part = [both[: 2 * quarter], both[2 * quarter :]]
        for n in range(2):
            part = [add(part[i], self.swap(part[i], self.wide[2 - 2 * i][n])) for i in range(2)]
        both = jnp.concatenate(part)
        for step in reversed(self.mid):
            both = join(both, self.swap(both, step), step[0])
        both = both.reshape(4, 4, quarter, cols)
        chunks = [both[:, k].reshape(4 * quarter, cols) for k in range(4)]
        for n in (1, 0):
            chunks = [join(c, self.swap(c, w[n]), w[n][0]) for c, w in zip(chunks, self.wide)]
        part = [jnp.concatenate([chunks[i], chunks[2 + i]]) for i in range(2)]
        return part, [lax.ppermute(p, "dp", self.other_core) for p in part]


def finish_kernel(factor, core_ref, q_mine, k_mine, v_mine, o_mine, q_oth, k_oth, v_oth, o_oth, *outs):
    core = core_ref[0]

    def write(q, k, v, o):
        for src, out in zip((q, k, v), outs):
            out[...] = src[...].T.astype(F32) * factor
        outs[3][...] = o[...].astype(F32) * factor

    @pl.when(core == 0)
    def _():
        write(q_mine, k_mine, v_oth, o_oth)

    @pl.when(core != 0)
    def _():
        write(q_oth, k_oth, v_mine, o_mine)


def finish(core, part, other, factor):
    size = part[0].shape[0]
    wide = pl.BlockSpec((BLOCK, size), lambda i, c: (i, 0))

    def taken(first, tall):
        def at(i, c):
            row = jnp.where(c[0] == first, i, 0)
            return (0, row) if tall else (row, 0)

        return pl.BlockSpec((size, BLOCK) if tall else (BLOCK, size), at)

    specs = [taken(f, t) for f, t in ((0, 1), (0, 1), (1, 1), (1, 0))]
    specs += [taken(f, t) for f, t in ((1, 1), (1, 1), (0, 1), (0, 0))]
    args = [part[0], part[1], part[0], part[1], other[0], other[1], other[0], other[1]]
    return pl.pallas_call(
        functools.partial(finish_kernel, factor),
        out_shape=[jax.ShapeDtypeStruct((size, size), F32)] * 4,
        grid_spec=pltpu.PrefetchScalarGridSpec(
            num_scalar_prefetch=1,
            grid=(size // BLOCK,),
            in_specs=specs,
            out_specs=[wide] * 4,
        ),
        name="finish",
    )(core.reshape(1), *args)


def local(
    vertex_embeddings,
    incoming_adjoint,
    asking_projector_matrix,
    lookup_projector_matrix,
    content_projector_matrix,
    final_projector_matrix,
    grouped_vertex_permutation,
    listed_tiles,
    active_tile_tally,
):
    rows = vertex_embeddings[0]
    cotan = incoming_adjoint[0]
    parts = lax.axis_size("node")
    halves = H // parts
    cut = parts * HD
    width = rows.shape[0]
    total = parts * width

    def swap(arr):
        return lax.all_to_all(arr, "node", split_axis=0, concat_axis=0, tiled=True)

    me = lax.axis_index("node")
    order = grouped_vertex_permutation[0]
    dims_first = (((0,), (0,)), ((), ()))
    dims_back = (((0,), (1,)), ((), ()))
    arrived = []
    for n in range(halves):
        own = slice(n * cut, (n + 1) * cut)
        sent = [
            project(asking_projector_matrix[:, own], rows),
            project(lookup_projector_matrix[:, own], rows),
            project(content_projector_matrix[:, own], rows),
            dot(final_projector_matrix[own], cotan, NT).astype(BF16),
        ]
        part = jnp.stack([t.reshape(parts, HD, width) for t in sent], axis=1)
        arrived.append(swap(part.reshape(parts, 4 * HD, width)))
    done = []
    for n in range(halves):
        head = n * parts + me
        ids = lax.dynamic_index_in_dim(listed_tiles[0], head, 0, keepdims=False)
        live = lax.dynamic_index_in_dim(active_tile_tally[0], head, 0, keepdims=False)
        done.append(attend_head(order, ids, live, arrived[n]))
    first, done[1] = lax.optimization_barrier((swap(done[0]), done[1]))
    second = swap(done[1])

    def split(arr):
        arr = arr.reshape(parts, 4, HD, width)
        return [arr[:, i].reshape(cut, width) for i in range(4)]

    def grads_of(dk, dq, out, dv):
        pairs = ((dq, rows), (dk, rows), (dv, rows), (out, cotan))
        return [dot(a, b, NN).astype(BF16) for a, b in pairs]

    reduce = Sum()
    nodes = [split(first)]
    chunks, _ = reduce.start(0, grads_of(*nodes[0]))
    second, chunks = lax.optimization_barrier((second, chunks))
    nodes.append(split(second))
    dk, dq, out, dv = [jnp.concatenate(t, axis=0) for t in zip(*nodes)]
    result = lax.dot_general(
        out, final_projector_matrix, dims_first, preferred_element_type=jnp.float32
    ).astype(jnp.bfloat16)
    backward = (
        lax.dot_general(dq, asking_projector_matrix, dims_back, preferred_element_type=jnp.float32)
        + lax.dot_general(dk, lookup_projector_matrix, dims_back, preferred_element_type=jnp.float32)
        + lax.dot_general(dv, content_projector_matrix, dims_back, preferred_element_type=jnp.float32)
    ).astype(jnp.bfloat16)
    late, (result, backward) = reduce.start(1, grads_of(*nodes[1]), (result, backward))
    part, other = reduce.end(chunks + late)
    factor = 1.0 / math.sqrt(lax.axis_size("dp") * total)
    weights = finish(reduce.core, part, other, factor)
    return (result[None], backward[None], *weights)


def solution(mesh):
    placed = (
        P("dp", "node", None),
        P("dp", "node", None),
        P(),
        P(),
        P(),
        P(),
        P("dp", None),
        P("dp", None, None, None),
        P("dp", None, None),
    )
    return jax.shard_map(
        local,
        mesh=mesh,
        in_specs=placed,
        out_specs=(P("dp", "node", None), P("dp", "node", None), P(), P(), P(), P()),
        check_vma=False,
    )
```

```python
import functools
import math

import jax
import jax.numpy as jnp
from jax import lax
from jax.experimental import pallas as pl
from jax.experimental.pallas import tpu as pltpu
from jax.sharding import PartitionSpec as P


H = 32
HD = 24
BLOCK = 128
ROW_UNROLL = 64
GROUP = (4, 4, 4, 3)
LOG2E = math.log2(math.e)
F32 = jnp.float32
BF16 = jnp.bfloat16
NT = (((1,), (1,)), ((), ()))
NN = (((1,), (0,)), ((), ()))


def dot(a, b, dims):
    return lax.dot_general(a, b, dims, preferred_element_type=F32)


def eye():
    r = lax.broadcasted_iota(jnp.int32, (BLOCK, BLOCK), 0)
    c = lax.broadcasted_iota(jnp.int32, (BLOCK, BLOCK), 1)
    return jnp.where(r == c, 1.0, 0.0).astype(BF16)


def attend_kernel(
    nblocks,
    slots,
    per_source,
    order_ref,
    ids_ref,
    count_ref,
    in_ref,
    out_ref,
    rows_a,
    rows_b,
    x_rows,
    rhs_score,
    kv_cols,
    oq_cols,
    acc,
    bucket,
    fill,
):
    scale = 1.0 / math.sqrt(HD)
    pad = jnp.zeros((BLOCK - 4 * HD, BLOCK), F32)
    pad_half = jnp.zeros((BLOCK - 4 * HD, BLOCK), BF16)
    gap = jnp.zeros((HD, BLOCK), F32)
    ident = eye()

    def to_rows(j, _):
        src = j // per_source
        col = pl.multiple_of((j % per_source) * BLOCK, BLOCK)
        at = pl.multiple_of(j * BLOCK, BLOCK)
        tall = jnp.concatenate([in_ref[src, :, pl.ds(col, BLOCK)], pad_half], axis=0)
        rows_a[pl.ds(at, BLOCK), :] = tall.astype(F32).T
        return 0

    lax.fori_loop(0, nblocks, to_rows, 0, unroll=8)

    def fetch(i, _):
        base = pl.multiple_of(i * ROW_UNROLL, ROW_UNROLL)
        where = order_ref.at[pl.ds(base, ROW_UNROLL)]
        for u in range(ROW_UNROLL):
            rows_b[pl.ds(base + u, 1), :] = rows_a[pl.ds(where[u], 1), :]
        return 0

    lax.fori_loop(0, nblocks * BLOCK // ROW_UNROLL, fetch, 0)

    def forms(j, _):
        at = pl.multiple_of(j * BLOCK, BLOCK)
        rows = rows_b[pl.ds(at, BLOCK), :]
        x_rows[j] = rows.astype(BF16)
        tall = rows.T
        q_t, up_t = tall[0:HD], tall[3 * HD : 4 * HD]
        score = jnp.concatenate([gap, q_t, gap, gap, pad], axis=0).astype(BF16)
        value = jnp.concatenate([gap, gap, up_t, gap, pad], axis=0).astype(BF16)
        rhs_score[j] = jnp.concatenate([score, value], axis=1)
        kv_cols[j] = tall[HD : 3 * HD].astype(BF16)
        acc[j] = jnp.zeros((BLOCK, BLOCK), F32)
        return 0

    lax.fori_loop(0, nblocks, forms, 0, unroll=8)

    for c in range(slots):
        fill[c] = 0

    def place(i, _):
        c = count_ref[i] - 1
        n = fill[c]
        bucket[c * nblocks + n] = i
        fill[c] = n + 1
        return 0

    lax.fori_loop(0, nblocks, place, 0)

    lane = lax.broadcasted_iota(jnp.int32, (BLOCK, BLOCK), 1)
    q_lanes = lane < HD
    up_lanes = (lane >= 3 * HD) & (lane < 4 * HD)

    def attend(items, live):
        where = [(b, [ids_ref[b * slots + m] for m in range(live)]) for b in items]
        both = []
        for b, ids in where:
            keys = jnp.concatenate([x_rows[j] for j in ids], axis=0)
            both.append(dot(keys, rhs_score[b], NN))
        back = []
        for s in both:
            score = s[:, :BLOCK]
            dprob = s[:, BLOCK:]
            top = jnp.max(score, axis=0, keepdims=True)
            expo = jnp.exp2((score - top) * (scale * LOG2E))
            prob = expo * (1.0 / jnp.sum(expo, axis=0, keepdims=True))
            delta = jnp.sum(prob * dprob, axis=0, keepdims=True)
            dscore = prob * (dprob - delta) * scale
            back.append(jnp.concatenate([dscore.astype(BF16), prob.astype(BF16)], axis=1))
        for (b, ids), g in zip(where, back):
            cols = jnp.concatenate([kv_cols[j] for j in ids], axis=1)
            oq = dot(cols, g, NN)
            oq_cols[b] = jnp.concatenate([oq[:HD, :BLOCK], oq[HD:, BLOCK:]], axis=0).astype(BF16)
        grads = []
        for (b, ids), g in zip(where, back):
            rows = x_rows[b]
            zero = jnp.zeros_like(rows)
            weight = jnp.concatenate(
                [jnp.where(q_lanes, rows, zero), jnp.where(up_lanes, rows, zero)], axis=0
            )
            grads.append(dot(g, weight, NN))
        for (b, ids), d in zip(where, grads):
            for m, j in enumerate(ids):
                acc[j] += d[m * BLOCK : (m + 1) * BLOCK]

    for c in range(slots):
        base = c * nblocks
        total = fill[c]

        def group(t, _, c=c, base=base):
            attend([bucket[base + GROUP[c] * t + u] for u in range(GROUP[c])], c + 1)
            return 0

        lax.fori_loop(0, total // GROUP[c], group, 0)

        def single(t, _, c=c, base=base):
            attend([bucket[base + t]], c + 1)
            return 0

        lax.fori_loop(total // GROUP[c] * GROUP[c], total, single, 0)

    def results(j, _):
        at = pl.multiple_of(j * BLOCK, BLOCK)
        oq = oq_cols[j].astype(F32)
        tall = jnp.concatenate([gap, oq, gap, pad], axis=0).astype(BF16)
        rows_b[pl.ds(at, BLOCK), :] = tall.astype(F32).T + acc[j]
        return 0

    lax.fori_loop(0, nblocks, results, 0, unroll=8)

    def put(i, _):
        base = pl.multiple_of(i * ROW_UNROLL, ROW_UNROLL)
        where = order_ref.at[pl.ds(base, ROW_UNROLL)]
        for u in range(ROW_UNROLL):
            rows_a[pl.ds(where[u], 1), :] = rows_b[pl.ds(base + u, 1), :]
        return 0

    lax.fori_loop(0, nblocks * BLOCK // ROW_UNROLL, put, 0)

    def to_cols(j, _):
        dst = j // per_source
        col = pl.multiple_of((j % per_source) * BLOCK, BLOCK)
        at = pl.multiple_of(j * BLOCK, BLOCK)
        tall = rows_a[pl.ds(at, BLOCK), :].T
        out_ref[dst, :, pl.ds(col, BLOCK)] = tall[: 4 * HD].astype(BF16)
        return 0

    lax.fori_loop(0, nblocks, to_cols, 0, unroll=8)


def attend_head(order, ids, counts, arrived):
    sources, feats, width = arrived.shape
    total = sources * width
    nblocks = total // BLOCK
    slots = ids.shape[-1]
    smem = pl.BlockSpec(memory_space=pltpu.SMEM)
    vmem = pl.BlockSpec(memory_space=pltpu.VMEM)
    return pl.pallas_call(
        functools.partial(attend_kernel, nblocks, slots, width // BLOCK),
        out_shape=jax.ShapeDtypeStruct((sources, feats, width), BF16),
        in_specs=[smem] * 3 + [vmem],
        out_specs=vmem,
        scratch_shapes=[
            pltpu.VMEM((total, BLOCK), F32),
            pltpu.VMEM((total, BLOCK), F32),
            pltpu.VMEM((nblocks, BLOCK, BLOCK), BF16),
            pltpu.VMEM((nblocks, BLOCK, 2 * BLOCK), BF16),
            pltpu.VMEM((nblocks, 2 * HD, BLOCK), BF16),
            pltpu.VMEM((nblocks, 2 * HD, BLOCK), BF16),
            pltpu.VMEM((nblocks, BLOCK, BLOCK), F32),
            pltpu.SMEM((slots * nblocks,), jnp.int32),
            pltpu.SMEM((slots,), jnp.int32),
        ],
        compiler_params=pltpu.CompilerParams(vmem_limit_bytes=40000 * 1024),
        cost_estimate=pl.CostEstimate(
            flops=30_000_000_000, bytes_accessed=100_000_000, transcendentals=0
        ),
        name="attend",
    )(order, ids.reshape(-1), counts, arrived)


def project(weight, rows):
    return lax.dot_general(
        weight, rows, (((0,), (1,)), ((), ())), preferred_element_type=jnp.float32
    ).astype(jnp.bfloat16)


def ring(axis_name, size, to_coord, to_index, flip):
    pairs = []
    for i in range(size):
        c = to_coord(i)
        pairs.append((i, to_index(i, 3 - c if flip else c ^ 1)))
    return axis_name, pairs


def torus(dp, node):
    side = 4
    z = lambda i: i // 2
    x = lambda i: i // side
    y = lambda i: i % side
    axes = {
        "z": ("dp", z, lambda i, c: c * 2 + i % 2),
        "x": ("node", x, lambda i, c: c * side + i % side),
        "y": ("node", y, lambda i, c: (i // side) * side + c),
    }
    sizes = {"dp": dp, "node": node}
    out = {}
    for key, (name, coord, index) in axes.items():
        pairings = [ring(name, sizes[name], coord, index, flip) for flip in (False, True)]
        out[key] = (coord(lax.axis_index(name)), pairings)
    return out


def pick(arr, bit):
    two = arr.reshape(2, arr.shape[0] // 2, arr.shape[1])
    return jnp.where(bit == 0, two[0], two[1])


def join(mine, other, bit):
    low = jnp.where(bit == 0, mine, other)
    high = jnp.where(bit == 0, other, mine)
    return jnp.concatenate([low, high], axis=0)


def add(a, b):
    return (a.astype(F32) + b.astype(F32)).astype(BF16)


class Sum:
    def __init__(self):
        self.dp, node = lax.axis_size("dp"), lax.axis_size("node")
        axes = torus(self.dp, node)
        self.core = lax.axis_index("dp") % 2
        self.other_core = [(i, i ^ 1) for i in range(self.dp)]

        def plan(key):
            coord, pairings = axes[key]
            low = ((coord == 1) | (coord == 2)).astype(jnp.int32)
            return list(zip((low, (coord >= 2).astype(jnp.int32)), pairings))

        wide = [plan("z"), plan("x")]
        self.wide = [p[::-1] if m else p for p in wide for m in range(2)]
        self.mid = plan("y")

    def swap(self, arr, step):
        return lax.ppermute(arr, step[1][0], step[1][1])

    def halve(self, arr, step):
        return pick(arr, step[0]), self.swap(pick(arr, 1 - step[0]), step)

    def meet(self, grads):
        low, high = [jnp.concatenate(grads[i : i + 2]) for i in (0, 2)]
        send = jnp.where(self.core == 0, high, low)
        keep = jnp.where(self.core == 0, low, high)
        return add(keep, lax.ppermute(send, "dp", self.other_core))

    def start(self, totals, also):
        deep = totals[0].shape[0] // 2
        chunks = [t[m * deep : (m + 1) * deep] for t in totals for m in range(2)]
        for n in range(2):
            pairs = [self.halve(c, w[n]) for c, w in zip(chunks, self.wide)]
            if n == 0:
                pairs[3], also = lax.optimization_barrier((pairs[3], also))
            chunks = [add(*p) for p in pairs]
        return chunks, also

    def end(self, chunks):
        cols = chunks[0].shape[1]
        quarter = chunks[0].shape[0] // 4
        both = jnp.stack([c.reshape(4, quarter, cols) for c in chunks], axis=1)
        both = both.reshape(16 * quarter, cols)
        for step in self.mid:
            both = add(*self.halve(both, step))
        part = [both[: 2 * quarter], both[2 * quarter :]]
        for n in range(2):
            part = [add(part[i], self.swap(part[i], self.wide[2 - 2 * i][n])) for i in range(2)]
        both = jnp.concatenate(part)
        for step in reversed(self.mid):
            both = join(both, self.swap(both, step), step[0])
        both = both.reshape(4, 4, quarter, cols)
        chunks = [both[:, k].reshape(4 * quarter, cols) for k in range(4)]
        for n in (1, 0):
            chunks = [join(c, self.swap(c, w[n]), w[n][0]) for c, w in zip(chunks, self.wide)]
        part = [jnp.concatenate([chunks[i], chunks[2 + i]]) for i in range(2)]
        return part, [lax.ppermute(p, "dp", self.other_core) for p in part]


def finish_kernel(factor, core_ref, q_mine, k_mine, v_mine, o_mine, q_oth, k_oth, v_oth, o_oth, *outs):
    core = core_ref[0]

    def write(q, k, v, o):
        for src, out in zip((q, k, v), outs):
            out[...] = src[...].T.astype(F32) * factor
        outs[3][...] = o[...].astype(F32) * factor

    @pl.when(core == 0)
    def _():
        write(q_mine, k_mine, v_oth, o_oth)

    @pl.when(core != 0)
    def _():
        write(q_oth, k_oth, v_mine, o_mine)


def finish(core, part, other, factor):
    size = part[0].shape[0]
    wide = pl.BlockSpec((BLOCK, size), lambda i, c: (i, 0))

    def taken(first, tall):
        def at(i, c):
            row = jnp.where(c[0] == first, i, 0)
            return (0, row) if tall else (row, 0)

        return pl.BlockSpec((size, BLOCK) if tall else (BLOCK, size), at)

    specs = [taken(f, t) for f, t in ((0, 1), (0, 1), (1, 1), (1, 0))]
    specs += [taken(f, t) for f, t in ((1, 1), (1, 1), (0, 1), (0, 0))]
    args = [part[0], part[1], part[0], part[1], other[0], other[1], other[0], other[1]]
    return pl.pallas_call(
        functools.partial(finish_kernel, factor),
        out_shape=[jax.ShapeDtypeStruct((size, size), F32)] * 4,
        grid_spec=pltpu.PrefetchScalarGridSpec(
            num_scalar_prefetch=1,
            grid=(size // BLOCK,),
            in_specs=specs,
            out_specs=[wide] * 4,
        ),
        name="finish",
    )(core.reshape(1), *args)


def local(
    vertex_embeddings,
    incoming_adjoint,
    asking_projector_matrix,
    lookup_projector_matrix,
    content_projector_matrix,
    final_projector_matrix,
    grouped_vertex_permutation,
    listed_tiles,
    active_tile_tally,
):
    rows = vertex_embeddings[0]
    cotan = incoming_adjoint[0]
    parts = lax.axis_size("node")
    halves = H // parts
    cut = parts * HD
    width = rows.shape[0]
    total = parts * width

    def swap(arr):
        return lax.all_to_all(arr, "node", split_axis=0, concat_axis=0, tiled=True)

    me = lax.axis_index("node")
    order = grouped_vertex_permutation[0]
    dims_first = (((0,), (0,)), ((), ()))
    dims_back = (((0,), (1,)), ((), ()))
    arrived = []
    for n in range(halves):
        own = slice(n * cut, (n + 1) * cut)
        sent = [
            project(asking_projector_matrix[:, own], rows),
            project(lookup_projector_matrix[:, own], rows),
            project(content_projector_matrix[:, own], rows),
            dot(final_projector_matrix[own], cotan, NT).astype(BF16),
        ]
        part = jnp.stack([t.reshape(parts, HD, width) for t in sent], axis=1)
        arrived.append(swap(part.reshape(parts, 4 * HD, width)))
    done = []
    for n in range(halves):
        head = n * parts + me
        ids = lax.dynamic_index_in_dim(listed_tiles[0], head, 0, keepdims=False)
        live = lax.dynamic_index_in_dim(active_tile_tally[0], head, 0, keepdims=False)
        done.append(attend_head(order, ids, live, arrived[n]))
    first, done[1] = lax.optimization_barrier((swap(done[0]), done[1]))
    second = swap(done[1])

    def split(arr):
        arr = arr.reshape(parts, 4, HD, width)
        return [arr[:, i].reshape(cut, width) for i in range(4)]

    def grads_of(dk, dq, out, dv):
        pairs = ((dq, rows), (dk, rows), (dv, rows), (out, cotan))
        return [dot(a, b, NN).astype(BF16) for a, b in pairs]

    reduce = Sum()
    nodes = [split(first)]
    total0 = reduce.meet(grads_of(*nodes[0]))
    second, total0 = lax.optimization_barrier((second, total0))
    nodes.append(split(second))
    dk, dq, out, dv = [jnp.concatenate(t, axis=0) for t in zip(*nodes)]
    result = lax.dot_general(
        out, final_projector_matrix, dims_first, preferred_element_type=jnp.float32
    ).astype(jnp.bfloat16)
    backward = (
        lax.dot_general(dq, asking_projector_matrix, dims_back, preferred_element_type=jnp.float32)
        + lax.dot_general(dk, lookup_projector_matrix, dims_back, preferred_element_type=jnp.float32)
        + lax.dot_general(dv, content_projector_matrix, dims_back, preferred_element_type=jnp.float32)
    ).astype(jnp.bfloat16)
    totals = [total0, reduce.meet(grads_of(*nodes[1]))]
    chunks, (result, backward) = reduce.start(totals, (result, backward))
    part, other = reduce.end(chunks)
    factor = 1.0 / math.sqrt(lax.axis_size("dp") * total)
    weights = finish(reduce.core, part, other, factor)
    return (result[None], backward[None], *weights)


def solution(mesh):
    placed = (
        P("dp", "node", None),
        P("dp", "node", None),
        P(),
        P(),
        P(),
        P(),
        P("dp", None),
        P("dp", None, None, None),
        P("dp", None, None),
    )
    return jax.shard_map(
        local,
        mesh=mesh,
        in_specs=placed,
        out_specs=(P("dp", "node", None), P("dp", "node", None), P(), P(), P(), P()),
        check_vma=False,
    )
```

```python
import functools
import math

import jax
import jax.numpy as jnp
from jax import lax
from jax.experimental import pallas as pl
from jax.experimental.pallas import tpu as pltpu
from jax.sharding import PartitionSpec as P

H = 32
HD = 24
BLOCK = 128
ROW_UNROLL = 64
FINISH_BLOCK = 384
GROUP = (4, 4, 4, 3)
LOG2E = math.log2(math.e)
F32 = jnp.float32
BF16 = jnp.bfloat16
NT = (((1,), (1,)), ((), ()))
NN = (((1,), (0,)), ((), ()))


def dot(a, b, dims):
    return lax.dot_general(a, b, dims, preferred_element_type=F32)


def eye():
    r = lax.broadcasted_iota(jnp.int32, (BLOCK, BLOCK), 0)
    c = lax.broadcasted_iota(jnp.int32, (BLOCK, BLOCK), 1)
    return jnp.where(r == c, 1.0, 0.0).astype(BF16)


def attend_kernel(
    nblocks,
    slots,
    per_source,
    order_ref,
    ids_ref,
    count_ref,
    in_ref,
    out_ref,
    rows_a,
    rows_b,
    x_rows,
    rhs_score,
    kv_cols,
    oq_cols,
    acc,
    bucket,
    fill,
):
    scale = 1.0 / math.sqrt(HD)
    pad = jnp.zeros((BLOCK - 4 * HD, BLOCK), F32)
    pad_half = jnp.zeros((BLOCK - 4 * HD, BLOCK), BF16)
    gap = jnp.zeros((HD, BLOCK), F32)
    ident = eye()

    def to_rows(j, _):
        src = j // per_source
        col = pl.multiple_of((j % per_source) * BLOCK, BLOCK)
        at = pl.multiple_of(j * BLOCK, BLOCK)
        tall = jnp.concatenate([in_ref[src, :, pl.ds(col, BLOCK)], pad_half], axis=0)
        rows_a[pl.ds(at, BLOCK), :] = tall.astype(F32).T
        return 0

    lax.fori_loop(0, nblocks, to_rows, 0, unroll=8)

    def fetch(i, _):
        base = pl.multiple_of(i * ROW_UNROLL, ROW_UNROLL)
        where = order_ref.at[pl.ds(base, ROW_UNROLL)]
        for u in range(ROW_UNROLL):
            rows_b[pl.ds(base + u, 1), :] = rows_a[pl.ds(where[u], 1), :]
        return 0

    lax.fori_loop(0, nblocks * BLOCK // ROW_UNROLL, fetch, 0)

    def forms(j, _):
        at = pl.multiple_of(j * BLOCK, BLOCK)
        rows = rows_b[pl.ds(at, BLOCK), :]
        x_rows[j] = rows.astype(BF16)
        tall = rows.T
        q_t, up_t = tall[0:HD], tall[3 * HD : 4 * HD]
        score = jnp.concatenate([gap, q_t, gap, gap, pad], axis=0).astype(BF16)
        value = jnp.concatenate([gap, gap, up_t, gap, pad], axis=0).astype(BF16)
        rhs_score[j] = jnp.concatenate([score, value], axis=1)
        kv_cols[j] = tall[HD : 3 * HD].astype(BF16)
        acc[j] = jnp.zeros((BLOCK, BLOCK), F32)
        return 0

    lax.fori_loop(0, nblocks, forms, 0, unroll=8)

    for c in range(slots):
        fill[c] = 0

    def place(i, _):
        c = count_ref[i] - 1
        n = fill[c]
        bucket[c * nblocks + n] = i
        fill[c] = n + 1
        return 0

    lax.fori_loop(0, nblocks, place, 0)

    lane = lax.broadcasted_iota(jnp.int32, (BLOCK, BLOCK), 1)
    q_lanes = lane < HD
    up_lanes = (lane >= 3 * HD) & (lane < 4 * HD)

    def attend(items, live):
        where = [(b, [ids_ref[b * slots + m] for m in range(live)]) for b in items]
        both = []
        for b, ids in where:
            keys = jnp.concatenate([x_rows[j] for j in ids], axis=0)
            both.append(dot(keys, rhs_score[b], NN))
        back = []
        for s in both:
            score = s[:, :BLOCK]
            dprob = s[:, BLOCK:]
            top = jnp.max(score, axis=0, keepdims=True)
            expo = jnp.exp2((score - top) * (scale * LOG2E))
            prob = expo * (1.0 / jnp.sum(expo, axis=0, keepdims=True))
            delta = jnp.sum(prob * dprob, axis=0, keepdims=True)
            dscore = prob * (dprob - delta) * scale
            back.append(jnp.concatenate([dscore.astype(BF16), prob.astype(BF16)], axis=1))
        for (b, ids), g in zip(where, back):
            cols = jnp.concatenate([kv_cols[j] for j in ids], axis=1)
            oq = dot(cols, g, NN)
            oq_cols[b] = jnp.concatenate([oq[:HD, :BLOCK], oq[HD:, BLOCK:]], axis=0).astype(BF16)
        grads = []
        for (b, ids), g in zip(where, back):
            rows = x_rows[b]
            zero = jnp.zeros_like(rows)
            weight = jnp.concatenate(
                [jnp.where(q_lanes, rows, zero), jnp.where(up_lanes, rows, zero)], axis=0
            )
            grads.append(dot(g, weight, NN))
        for (b, ids), d in zip(where, grads):
            for m, j in enumerate(ids):
                acc[j] += d[m * BLOCK : (m + 1) * BLOCK]

    for c in range(slots):
        base = c * nblocks
        total = fill[c]

        def group(t, _, c=c, base=base):
            attend([bucket[base + GROUP[c] * t + u] for u in range(GROUP[c])], c + 1)
            return 0

        lax.fori_loop(0, total // GROUP[c], group, 0)

        def single(t, _, c=c, base=base):
            attend([bucket[base + t]], c + 1)
            return 0

        lax.fori_loop(total // GROUP[c] * GROUP[c], total, single, 0)

    def results(j, _):
        at = pl.multiple_of(j * BLOCK, BLOCK)
        oq = oq_cols[j].astype(F32)
        tall = jnp.concatenate([gap, oq, gap, pad], axis=0).astype(BF16)
        rows_b[pl.ds(at, BLOCK), :] = tall.astype(F32).T + acc[j]
        return 0

    lax.fori_loop(0, nblocks, results, 0, unroll=8)

    def put(i, _):
        base = pl.multiple_of(i * ROW_UNROLL, ROW_UNROLL)
        where = order_ref.at[pl.ds(base, ROW_UNROLL)]
        for u in range(ROW_UNROLL):
            rows_a[pl.ds(where[u], 1), :] = rows_b[pl.ds(base + u, 1), :]
        return 0

    lax.fori_loop(0, nblocks * BLOCK // ROW_UNROLL, put, 0)

    def to_cols(j, _):
        dst = j // per_source
        col = pl.multiple_of((j % per_source) * BLOCK, BLOCK)
        at = pl.multiple_of(j * BLOCK, BLOCK)
        tall = rows_a[pl.ds(at, BLOCK), :].T
        out_ref[dst, :, pl.ds(col, BLOCK)] = tall[: 4 * HD].astype(BF16)
        return 0

    lax.fori_loop(0, nblocks, to_cols, 0, unroll=8)


def attend_head(order, ids, counts, arrived):
    sources, feats, width = arrived.shape
    total = sources * width
    nblocks = total // BLOCK
    slots = ids.shape[-1]
    smem = pl.BlockSpec(memory_space=pltpu.SMEM)
    vmem = pl.BlockSpec(memory_space=pltpu.VMEM)
    return pl.pallas_call(
        functools.partial(attend_kernel, nblocks, slots, width // BLOCK),
        out_shape=jax.ShapeDtypeStruct((sources, feats, width), BF16),
        in_specs=[smem] * 3 + [vmem],
        out_specs=vmem,
        scratch_shapes=[
            pltpu.VMEM((total, BLOCK), F32),
            pltpu.VMEM((total, BLOCK), F32),
            pltpu.VMEM((nblocks, BLOCK, BLOCK), BF16),
            pltpu.VMEM((nblocks, BLOCK, 2 * BLOCK), BF16),
            pltpu.VMEM((nblocks, 2 * HD, BLOCK), BF16),
            pltpu.VMEM((nblocks, 2 * HD, BLOCK), BF16),
            pltpu.VMEM((nblocks, BLOCK, BLOCK), F32),
            pltpu.SMEM((slots * nblocks,), jnp.int32),
            pltpu.SMEM((slots,), jnp.int32),
        ],
        compiler_params=pltpu.CompilerParams(vmem_limit_bytes=40000 * 1024),
        cost_estimate=pl.CostEstimate(
            flops=30_000_000_000, bytes_accessed=100_000_000, transcendentals=0
        ),
        name="attend",
    )(order, ids.reshape(-1), counts, arrived)


def project(weight, rows):
    return lax.dot_general(
        weight, rows, (((0,), (1,)), ((), ())), preferred_element_type=jnp.float32
    ).astype(jnp.bfloat16)


def ring(axis_name, size, to_coord, to_index, flip):
    pairs = []
    for i in range(size):
        c = to_coord(i)
        pairs.append((i, to_index(i, 3 - c if flip else c ^ 1)))
    return axis_name, pairs


def torus(dp, node):
    side = 4
    z = lambda i: i // 2
    x = lambda i: i // side
    y = lambda i: i % side
    axes = {
        "z": ("dp", z, lambda i, c: c * 2 + i % 2),
        "x": ("node", x, lambda i, c: c * side + i % side),
        "y": ("node", y, lambda i, c: (i // side) * side + c),
    }
    sizes = {"dp": dp, "node": node}
    out = {}
    for key, (name, coord, index) in axes.items():
        pairings = [ring(name, sizes[name], coord, index, flip) for flip in (False, True)]
        out[key] = (coord(lax.axis_index(name)), pairings)
    return out


def pick(arr, bit):
    two = arr.reshape(2, arr.shape[0] // 2, arr.shape[1])
    return jnp.where(bit == 0, two[0], two[1])


def join(mine, other, bit):
    low = jnp.where(bit == 0, mine, other)
    high = jnp.where(bit == 0, other, mine)
    return jnp.concatenate([low, high], axis=0)


def add(a, b):
    return (a.astype(F32) + b.astype(F32)).astype(BF16)


def all_reduce(grads, also):
    dp, node = lax.axis_size("dp"), lax.axis_size("node")
    axes = torus(dp, node)
    core = lax.axis_index("dp") % 2
    other_core = [(i, i ^ 1) for i in range(dp)]

    def plan(key):
        coord, pairings = axes[key]
        keep_high = (((coord == 1) | (coord == 2)).astype(jnp.int32), (coord >= 2).astype(jnp.int32))
        return list(zip(keep_high, pairings))

    def swap(arr, step):
        return lax.ppermute(arr, step[1][0], step[1][1])

    def halve(arr, step):
        return pick(arr, step[0]), swap(pick(arr, 1 - step[0]), step)

    send = [jnp.where(core == 0, grads[2 + i], grads[i]) for i in range(2)]
    keep = [jnp.where(core == 0, grads[i], grads[2 + i]) for i in range(2)]
    part = [add(k, lax.ppermute(s, "dp", other_core)) for k, s in zip(keep, send)]
    wide = [plan("x"), plan("z")]
    wide = [p[::-1] if m else p for p in wide for m in range(2)]
    mid = plan("y")
    deep = part[0].shape[0] // 2
    cols = part[0].shape[1]
    chunks = [p[m * deep : (m + 1) * deep] for p in part for m in range(2)]
    def together(arrs, steps, also=None):
        arrs = lax.optimization_barrier(arrs)
        got = [swap(t, s) for t, s in zip(arrs, steps)]
        return lax.optimization_barrier((got, also))

    for n in range(2):
        steps = [w[n] for w in wide]
        sent = [pick(c, 1 - s[0]) for c, s in zip(chunks, steps)]
        got, also = together(sent, steps, also)
        chunks = [add(pick(c, s[0]), g) for c, s, g in zip(chunks, steps, got)]
    quarter = chunks[0].shape[0] // 4
    both = jnp.stack([c.reshape(4, quarter, cols) for c in chunks], axis=1)
    both = both.reshape(16 * quarter, cols)
    for step in mid:
        both = add(*halve(both, step))
    part = [both[: 2 * quarter], both[2 * quarter :]]
    for n in range(2):
        got, _ = together(part, [wide[2 - 2 * i][n] for i in range(2)])
        part = [add(p, g) for p, g in zip(part, got)]
    both = jnp.concatenate(part)
    for step in reversed(mid):
        both = join(both, swap(both, step), step[0])
    both = both.reshape(4, 4, quarter, cols)
    chunks = [both[:, k].reshape(4 * quarter, cols) for k in range(4)]
    for n in (1, 0):
        steps = [w[n] for w in wide]
        got, _ = together(chunks, steps)
        chunks = [join(c, g, s[0]) for c, g, s in zip(chunks, got, steps)]
    part = [jnp.concatenate(chunks[2 * i : 2 * i + 2]) for i in range(2)]
    other = [lax.ppermute(p, "dp", other_core) for p in part]
    return core, part, other, also


def finish_kernel(factor, core_ref, q_mine, k_mine, v_mine, o_mine, q_oth, k_oth, v_oth, o_oth, *outs):
    core = core_ref[0]

    def write(q, k, v, o):
        for src, out in zip((q, k, v), outs):
            out[...] = src[...].astype(F32).T * factor
        outs[3][...] = o[...].astype(F32) * factor

    @pl.when(core == 0)
    def _():
        write(q_mine, k_mine, v_oth, o_oth)

    @pl.when(core != 0)
    def _():
        write(q_oth, k_oth, v_mine, o_mine)


def finish(core, part, other, factor):
    size = part[0].shape[0]
    wide = pl.BlockSpec((FINISH_BLOCK, size), lambda i, c: (i, 0))

    def taken(first, tall):
        def at(i, c):
            row = jnp.where(c[0] == first, i, 0)
            return (0, row) if tall else (row, 0)

        return pl.BlockSpec((size, FINISH_BLOCK) if tall else (FINISH_BLOCK, size), at)

    specs = [taken(f, t) for f, t in ((0, 1), (0, 1), (1, 1), (1, 0))]
    specs += [taken(f, t) for f, t in ((1, 1), (1, 1), (0, 1), (0, 0))]
    args = [part[0], part[1], part[0], part[1], other[0], other[1], other[0], other[1]]
    return pl.pallas_call(
        functools.partial(finish_kernel, factor),
        out_shape=[jax.ShapeDtypeStruct((size, size), F32)] * 4,
        grid_spec=pltpu.PrefetchScalarGridSpec(
            num_scalar_prefetch=1,
            grid=(size // FINISH_BLOCK,),
            in_specs=specs,
            out_specs=[wide] * 4,
        ),
        name="finish",
    )(core.reshape(1), *args)


def local(
    vertex_embeddings,
    incoming_adjoint,
    asking_projector_matrix,
    lookup_projector_matrix,
    content_projector_matrix,
    final_projector_matrix,
    grouped_vertex_permutation,
    listed_tiles,
    active_tile_tally,
):
    rows = vertex_embeddings[0]
    cotan = incoming_adjoint[0]
    parts = lax.axis_size("node")
    halves = H // parts
    cut = parts * HD
    width = rows.shape[0]
    total = parts * width
    def swap(arr):
        return lax.all_to_all(arr, "node", split_axis=0, concat_axis=0, tiled=True)

    me = lax.axis_index("node")
    order = grouped_vertex_permutation[0]
    dims_first = (((0,), (0,)), ((), ()))
    dims_back = (((0,), (1,)), ((), ()))
    back = []
    for n in range(halves):
        own = slice(n * cut, (n + 1) * cut)
        sent = [
            project(asking_projector_matrix[:, own], rows),
            project(lookup_projector_matrix[:, own], rows),
            project(content_projector_matrix[:, own], rows),
            dot(final_projector_matrix[own], cotan, NT).astype(BF16),
        ]
        part = jnp.stack([t.reshape(parts, HD, width) for t in sent], axis=1)
        part = part.reshape(parts, 4 * HD, width)
        head = n * parts + me
        ids = lax.dynamic_index_in_dim(listed_tiles[0], head, 0, keepdims=False)
        live = lax.dynamic_index_in_dim(active_tile_tally[0], head, 0, keepdims=False)
        done = swap(attend_head(order, ids, live, swap(part))).reshape(parts, 4, HD, width)
        dk, dq, out, dv = [done[:, i].reshape(cut, width) for i in range(4)]
        back.append((dk, dq, out, dv))
    dk, dq, out, dv = [jnp.concatenate(t, axis=0) for t in zip(*back)]
    result = lax.dot_general(
        out, final_projector_matrix, dims_first, preferred_element_type=jnp.float32
    ).astype(jnp.bfloat16)
    backward = (
        lax.dot_general(dq, asking_projector_matrix, dims_back, preferred_element_type=jnp.float32)
        + lax.dot_general(dk, lookup_projector_matrix, dims_back, preferred_element_type=jnp.float32)
        + lax.dot_general(dv, content_projector_matrix, dims_back, preferred_element_type=jnp.float32)
    ).astype(jnp.bfloat16)
    factor = 1.0 / math.sqrt(lax.axis_size("dp") * total)
    grads = [
        lax.dot_general(a, b, dims, preferred_element_type=jnp.float32).astype(jnp.bfloat16)
        for a, b, dims in (
            (dq, rows, NN),
            (dk, rows, NN),
            (dv, rows, NN),
            (out, cotan, NN),
        )
    ]
    core, part, other, (result, backward) = all_reduce(grads, (result, backward))
    weights = finish(core, part, other, factor)
    return (result[None], backward[None], *weights)


def solution(mesh):
    placed = (
        P("dp", "node", None),
        P("dp", "node", None),
        P(),
        P(),
        P(),
        P(),
        P("dp", None),
        P("dp", None, None, None),
        P("dp", None, None),
    )
    return jax.shard_map(
        local,
        mesh=mesh,
        in_specs=placed,
        out_specs=(P("dp", "node", None), P("dp", "node", None), P(), P(), P(), P()),
        check_vma=False,
    )
```

```python
import functools
import math

import jax
import jax.numpy as jnp
from jax import lax
from jax.experimental import pallas as pl
from jax.experimental.pallas import tpu as pltpu
from jax.sharding import PartitionSpec as P

H = 32
HD = 24
BLOCK = 128
ROW_UNROLL = 64
FINISH_BLOCK = 384
GROUP = 4
LOG2E = math.log2(math.e)
F32 = jnp.float32
BF16 = jnp.bfloat16
NT = (((1,), (1,)), ((), ()))
NN = (((1,), (0,)), ((), ()))


def dot(a, b, dims):
    return lax.dot_general(a, b, dims, preferred_element_type=F32)


def eye():
    r = lax.broadcasted_iota(jnp.int32, (BLOCK, BLOCK), 0)
    c = lax.broadcasted_iota(jnp.int32, (BLOCK, BLOCK), 1)
    return jnp.where(r == c, 1.0, 0.0).astype(BF16)


def attend_kernel(
    nblocks,
    slots,
    per_source,
    order_ref,
    ids_ref,
    count_ref,
    in_ref,
    out_ref,
    rows_a,
    rows_b,
    x_rows,
    rhs_score,
    kv_cols,
    oq_cols,
    acc,
    bucket,
    fill,
):
    scale = 1.0 / math.sqrt(HD)
    pad = jnp.zeros((BLOCK - 4 * HD, BLOCK), F32)
    pad_half = jnp.zeros((BLOCK - 4 * HD, BLOCK), BF16)
    gap = jnp.zeros((HD, BLOCK), F32)
    ident = eye()

    def to_rows(j, _):
        src = j // per_source
        col = pl.multiple_of((j % per_source) * BLOCK, BLOCK)
        at = pl.multiple_of(j * BLOCK, BLOCK)
        tall = jnp.concatenate([in_ref[src, :, pl.ds(col, BLOCK)], pad_half], axis=0)
        rows_a[pl.ds(at, BLOCK), :] = tall.astype(F32).T
        return 0

    lax.fori_loop(0, nblocks, to_rows, 0, unroll=16)

    def fetch(i, _):
        base = pl.multiple_of(i * ROW_UNROLL, ROW_UNROLL)
        where = order_ref.at[pl.ds(base, ROW_UNROLL)]
        for u in range(ROW_UNROLL):
            rows_b[pl.ds(base + u, 1), :] = rows_a[pl.ds(where[u], 1), :]
        return 0

    lax.fori_loop(0, nblocks * BLOCK // ROW_UNROLL, fetch, 0)

    def forms(j, _):
        at = pl.multiple_of(j * BLOCK, BLOCK)
        rows = rows_b[pl.ds(at, BLOCK), :]
        x_rows[j] = rows.astype(BF16)
        tall = rows.T
        q_t, up_t = tall[0:HD], tall[3 * HD : 4 * HD]
        score = jnp.concatenate([gap, q_t, gap, gap, pad], axis=0).astype(BF16)
        value = jnp.concatenate([gap, gap, up_t, gap, pad], axis=0).astype(BF16)
        rhs_score[j] = jnp.concatenate([score, value], axis=1)
        kv_cols[j] = tall[HD : 3 * HD].astype(BF16)
        acc[j] = jnp.zeros((BLOCK, BLOCK), F32)
        return 0

    lax.fori_loop(0, nblocks, forms, 0, unroll=16)

    for c in range(slots):
        fill[c] = 0

    def place(i, _):
        c = count_ref[i] - 1
        n = fill[c]
        bucket[c * nblocks + n] = i
        fill[c] = n + 1
        return 0

    lax.fori_loop(0, nblocks, place, 0)

    lane = lax.broadcasted_iota(jnp.int32, (BLOCK, BLOCK), 1)
    q_lanes = lane < HD
    up_lanes = (lane >= 3 * HD) & (lane < 4 * HD)

    def attend(items, live):
        where = [(b, [ids_ref[b * slots + m] for m in range(live)]) for b in items]
        both = []
        for b, ids in where:
            keys = jnp.concatenate([x_rows[j] for j in ids], axis=0)
            both.append(dot(keys, rhs_score[b], NN))
        back = []
        for s in both:
            score = s[:, :BLOCK]
            dprob = s[:, BLOCK:]
            top = jnp.max(score, axis=0, keepdims=True)
            expo = jnp.exp2((score - top) * (scale * LOG2E))
            prob = expo * (1.0 / jnp.sum(expo, axis=0, keepdims=True))
            delta = jnp.sum(prob * dprob, axis=0, keepdims=True)
            dscore = prob * (dprob - delta) * scale
            back.append(jnp.concatenate([dscore.astype(BF16), prob.astype(BF16)], axis=1))
        for (b, ids), g in zip(where, back):
            cols = jnp.concatenate([kv_cols[j] for j in ids], axis=1)
            oq = dot(cols, g, NN)
            oq_cols[b] = jnp.concatenate([oq[:HD, :BLOCK], oq[HD:, BLOCK:]], axis=0).astype(BF16)
        grads = []
        for (b, ids), g in zip(where, back):
            rows = x_rows[b]
            zero = jnp.zeros_like(rows)
            weight = jnp.concatenate(
                [jnp.where(q_lanes, rows, zero), jnp.where(up_lanes, rows, zero)], axis=0
            )
            grads.append(dot(g, weight, NN))
        for (b, ids), d in zip(where, grads):
            for m, j in enumerate(ids):
                acc[j] += d[m * BLOCK : (m + 1) * BLOCK]

    for c in range(slots):
        base = c * nblocks
        total = fill[c]

        def group(t, _, c=c, base=base):
            attend([bucket[base + GROUP * t + u] for u in range(GROUP)], c + 1)
            return 0

        lax.fori_loop(0, total // GROUP, group, 0)

        def single(t, _, c=c, base=base):
            attend([bucket[base + t]], c + 1)
            return 0

        lax.fori_loop(total // GROUP * GROUP, total, single, 0)

    def results(j, _):
        at = pl.multiple_of(j * BLOCK, BLOCK)
        oq = oq_cols[j].astype(F32)
        tall = jnp.concatenate([gap, oq, gap, pad], axis=0).astype(BF16)
        rows_b[pl.ds(at, BLOCK), :] = tall.astype(F32).T + acc[j]
        return 0

    lax.fori_loop(0, nblocks, results, 0, unroll=16)

    def put(i, _):
        base = pl.multiple_of(i * ROW_UNROLL, ROW_UNROLL)
        where = order_ref.at[pl.ds(base, ROW_UNROLL)]
        for u in range(ROW_UNROLL):
            rows_a[pl.ds(where[u], 1), :] = rows_b[pl.ds(base + u, 1), :]
        return 0

    lax.fori_loop(0, nblocks * BLOCK // ROW_UNROLL, put, 0)

    def to_cols(j, _):
        dst = j // per_source
        col = pl.multiple_of((j % per_source) * BLOCK, BLOCK)
        at = pl.multiple_of(j * BLOCK, BLOCK)
        tall = rows_a[pl.ds(at, BLOCK), :].T
        out_ref[dst, :, pl.ds(col, BLOCK)] = tall[: 4 * HD].astype(BF16)
        return 0

    lax.fori_loop(0, nblocks, to_cols, 0, unroll=16)


def attend_head(order, ids, counts, arrived):
    sources, feats, width = arrived.shape
    total = sources * width
    nblocks = total // BLOCK
    slots = ids.shape[-1]
    smem = pl.BlockSpec(memory_space=pltpu.SMEM)
    vmem = pl.BlockSpec(memory_space=pltpu.VMEM)
    return pl.pallas_call(
        functools.partial(attend_kernel, nblocks, slots, width // BLOCK),
        out_shape=jax.ShapeDtypeStruct((sources, feats, width), BF16),
        in_specs=[smem] * 3 + [vmem],
        out_specs=vmem,
        scratch_shapes=[
            pltpu.VMEM((total, BLOCK), F32),
            pltpu.VMEM((total, BLOCK), F32),
            pltpu.VMEM((nblocks, BLOCK, BLOCK), BF16),
            pltpu.VMEM((nblocks, BLOCK, 2 * BLOCK), BF16),
            pltpu.VMEM((nblocks, 2 * HD, BLOCK), BF16),
            pltpu.VMEM((nblocks, 2 * HD, BLOCK), BF16),
            pltpu.VMEM((nblocks, BLOCK, BLOCK), F32),
            pltpu.SMEM((slots * nblocks,), jnp.int32),
            pltpu.SMEM((slots,), jnp.int32),
        ],
        compiler_params=pltpu.CompilerParams(vmem_limit_bytes=40000 * 1024),
        cost_estimate=pl.CostEstimate(
            flops=30_000_000_000, bytes_accessed=100_000_000, transcendentals=0
        ),
        name="attend",
    )(order, ids.reshape(-1), counts, arrived)


def project(weight, rows):
    return lax.dot_general(
        weight, rows, (((0,), (1,)), ((), ())), preferred_element_type=jnp.float32
    ).astype(jnp.bfloat16)


def ring(axis_name, size, to_coord, to_index, flip):
    pairs = []
    for i in range(size):
        c = to_coord(i)
        pairs.append((i, to_index(i, 3 - c if flip else c ^ 1)))
    return axis_name, pairs


def torus(dp, node):
    side = 4
    z = lambda i: i // 2
    x = lambda i: i // side
    y = lambda i: i % side
    axes = {
        "z": ("dp", z, lambda i, c: c * 2 + i % 2),
        "x": ("node", x, lambda i, c: c * side + i % side),
        "y": ("node", y, lambda i, c: (i // side) * side + c),
    }
    sizes = {"dp": dp, "node": node}
    out = {}
    for key, (name, coord, index) in axes.items():
        pairings = [ring(name, sizes[name], coord, index, flip) for flip in (False, True)]
        out[key] = (coord(lax.axis_index(name)), pairings)
    return out


def pick(arr, bit):
    two = arr.reshape(2, arr.shape[0] // 2, arr.shape[1])
    return jnp.where(bit == 0, two[0], two[1])


def join(mine, other, bit):
    low = jnp.where(bit == 0, mine, other)
    high = jnp.where(bit == 0, other, mine)
    return jnp.concatenate([low, high], axis=0)


def add(a, b):
    return (a.astype(F32) + b.astype(F32)).astype(BF16)


def all_reduce(grads, also):
    dp, node = lax.axis_size("dp"), lax.axis_size("node")
    axes = torus(dp, node)
    core = lax.axis_index("dp") % 2
    other_core = [(i, i ^ 1) for i in range(dp)]

    def plan(key):
        coord, pairings = axes[key]
        keep_high = (((coord == 1) | (coord == 2)).astype(jnp.int32), (coord >= 2).astype(jnp.int32))
        return list(zip(keep_high, pairings))

    def swap(arr, step):
        return lax.ppermute(arr, step[1][0], step[1][1])

    def halve(arr, step):
        return pick(arr, step[0]), swap(pick(arr, 1 - step[0]), step)

    send = [jnp.where(core == 0, grads[2 + i], grads[i]) for i in range(2)]
    keep = [jnp.where(core == 0, grads[i], grads[2 + i]) for i in range(2)]
    part = [add(k, lax.ppermute(s, "dp", other_core)) for k, s in zip(keep, send)]
    wide = [plan("x"), plan("z")]
    wide = [p[::-1] if m else p for p in wide for m in range(2)]
    mid = plan("y")
    deep = part[0].shape[0] // 2
    cols = part[0].shape[1]
    chunks = [p[m * deep : (m + 1) * deep] for p in part for m in range(2)]
    for n in range(2):
        pairs = [halve(c, w[n]) for c, w in zip(chunks, wide)]
        if n == 0:
            pairs[3], also = lax.optimization_barrier((pairs[3], also))
        chunks = [add(*p) for p in pairs]
    quarter = chunks[0].shape[0] // 4
    both = jnp.stack([c.reshape(4, quarter, cols) for c in chunks], axis=1)
    both = both.reshape(16 * quarter, cols)
    for step in mid:
        both = add(*halve(both, step))
    part = [both[: 2 * quarter], both[2 * quarter :]]
    for n in range(2):
        part = [add(part[i], swap(part[i], wide[2 - 2 * i][n])) for i in range(2)]
    both = jnp.concatenate(part)
    for step in reversed(mid):
        both = join(both, swap(both, step), step[0])
    both = both.reshape(4, 4, quarter, cols)
    chunks = [both[:, k].reshape(4 * quarter, cols) for k in range(4)]
    for n in (1, 0):
        chunks = [join(c, swap(c, w[n]), w[n][0]) for c, w in zip(chunks, wide)]
    part = [jnp.concatenate(chunks[2 * i : 2 * i + 2]) for i in range(2)]
    other = [lax.ppermute(p, "dp", other_core) for p in part]
    return core, part, other, also


def finish_kernel(factor, core_ref, q_mine, k_mine, v_mine, o_mine, q_oth, k_oth, v_oth, o_oth, *outs):
    core = core_ref[0]

    def write(q, k, v, o):
        for src, out in zip((q, k, v), outs):
            out[...] = src[...].astype(F32).T * factor
        outs[3][...] = o[...].astype(F32) * factor

    @pl.when(core == 0)
    def _():
        write(q_mine, k_mine, v_oth, o_oth)

    @pl.when(core != 0)
    def _():
        write(q_oth, k_oth, v_mine, o_mine)


def finish(core, part, other, factor):
    size = part[0].shape[0]
    wide = pl.BlockSpec((FINISH_BLOCK, size), lambda i, c: (i, 0))

    def taken(first, tall):
        def at(i, c):
            row = jnp.where(c[0] == first, i, 0)
            return (0, row) if tall else (row, 0)

        return pl.BlockSpec((size, FINISH_BLOCK) if tall else (FINISH_BLOCK, size), at)

    specs = [taken(f, t) for f, t in ((0, 1), (0, 1), (1, 1), (1, 0))]
    specs += [taken(f, t) for f, t in ((1, 1), (1, 1), (0, 1), (0, 0))]
    args = [part[0], part[1], part[0], part[1], other[0], other[1], other[0], other[1]]
    return pl.pallas_call(
        functools.partial(finish_kernel, factor),
        out_shape=[jax.ShapeDtypeStruct((size, size), F32)] * 4,
        grid_spec=pltpu.PrefetchScalarGridSpec(
            num_scalar_prefetch=1,
            grid=(size // FINISH_BLOCK,),
            in_specs=specs,
            out_specs=[wide] * 4,
        ),
        name="finish",
    )(core.reshape(1), *args)


def local(
    vertex_embeddings,
    incoming_adjoint,
    asking_projector_matrix,
    lookup_projector_matrix,
    content_projector_matrix,
    final_projector_matrix,
    grouped_vertex_permutation,
    listed_tiles,
    active_tile_tally,
):
    rows = vertex_embeddings[0]
    cotan = incoming_adjoint[0]
    parts = lax.axis_size("node")
    halves = H // parts
    cut = parts * HD
    width = rows.shape[0]
    total = parts * width
    def swap(arr):
        return lax.all_to_all(arr, "node", split_axis=0, concat_axis=0, tiled=True)

    me = lax.axis_index("node")
    order = grouped_vertex_permutation[0]
    dims_first = (((0,), (0,)), ((), ()))
    dims_back = (((0,), (1,)), ((), ()))
    back = []
    for n in range(halves):
        own = slice(n * cut, (n + 1) * cut)
        sent = [
            project(asking_projector_matrix[:, own], rows),
            project(lookup_projector_matrix[:, own], rows),
            project(content_projector_matrix[:, own], rows),
            dot(final_projector_matrix[own], cotan, NT).astype(BF16),
        ]
        part = jnp.stack([t.reshape(parts, HD, width) for t in sent], axis=1)
        part = part.reshape(parts, 4 * HD, width)
        head = n * parts + me
        ids = lax.dynamic_index_in_dim(listed_tiles[0], head, 0, keepdims=False)
        live = lax.dynamic_index_in_dim(active_tile_tally[0], head, 0, keepdims=False)
        done = swap(attend_head(order, ids, live, swap(part))).reshape(parts, 4, HD, width)
        dk, dq, out, dv = [done[:, i].reshape(cut, width) for i in range(4)]
        back.append((dk, dq, out, dv))
    dk, dq, out, dv = [jnp.concatenate(t, axis=0) for t in zip(*back)]
    result = lax.dot_general(
        out, final_projector_matrix, dims_first, preferred_element_type=jnp.float32
    ).astype(jnp.bfloat16)
    backward = (
        lax.dot_general(dq, asking_projector_matrix, dims_back, preferred_element_type=jnp.float32)
        + lax.dot_general(dk, lookup_projector_matrix, dims_back, preferred_element_type=jnp.float32)
        + lax.dot_general(dv, content_projector_matrix, dims_back, preferred_element_type=jnp.float32)
    ).astype(jnp.bfloat16)
    factor = 1.0 / math.sqrt(lax.axis_size("dp") * total)
    grads = [
        lax.dot_general(a, b, dims, preferred_element_type=jnp.float32).astype(jnp.bfloat16)
        for a, b, dims in (
            (dq, rows, NN),
            (dk, rows, NN),
            (dv, rows, NN),
            (out, cotan, NN),
        )
    ]
    core, part, other, (result, backward) = all_reduce(grads, (result, backward))
    weights = finish(core, part, other, factor)
    return (result[None], backward[None], *weights)


def solution(mesh):
    placed = (
        P("dp", "node", None),
        P("dp", "node", None),
        P(),
        P(),
        P(),
        P(),
        P("dp", None),
        P("dp", None, None, None),
        P("dp", None, None),
    )
    return jax.shard_map(
        local,
        mesh=mesh,
        in_specs=placed,
        out_specs=(P("dp", "node", None), P("dp", "node", None), P(), P(), P(), P()),
        check_vma=False,
    )
```
